32 devices in a mesh: dp: 8 (over z, y), tensor: 4 (over x, core).
Axes of the slice: x: 2, y: 2, z: 4, core: 2. Of those that a mesh axis runs over, the one named last changes fastest.
Arguments:
- tokens: bfloat16 [4096, 768], P(('dp', 'tensor')), may hold values from -6 to 6
- segments: int32 [4096], P('dp'), may hold values from 0 to 8, as said below
- positions: int32 [4096], P('dp'), may hold values from 0 to 511, as said below
- ln1_gain: float32 [1, 768], replicated, may hold values from 0.5 to 1.5
- ln1_bias: float32 [1, 768], replicated, may hold values from -1.5 to 1.5
- ln2_gain: float32 [1, 768], replicated, may hold values from 0.5 to 1.5
- ln2_bias: float32 [1, 768], replicated, may hold values from -1.5 to 1.5
- qkv_weight: bfloat16 [1, 768, 2304], P(None, 'dp', 'tensor')
- qkv_bias: float32 [1, 2304], P(None, 'tensor'), may hold values from -1.5 to 1.5
- dense_weight: bfloat16 [1, 768, 768], P(None, 'tensor', 'dp'), may hold values from -0.875 to 0.875
- dense_bias: float32 [1, 768], replicated, may hold values from -2.5 to 2.5
- fc1_weight: bfloat16 [1, 768, 3072], P(None, 'dp', 'tensor'), may hold values from -0.21875 to 0.21875
- fc1_bias: float32 [1, 3072], P(None, 'tensor'), may hold values from -2.5 to 2.5
- fc2_weight: bfloat16 [1, 3072, 768], P(None, 'tensor', 'dp'), may hold values from -0.109375 to 0.109375
- fc2_bias: float32 [1, 768], replicated, may hold values from -2.5 to 2.5
- cotangent: bfloat16 [4096, 768], P(('dp', 'tensor')), may hold values from -6 to 6
Outputs:
- y_out: float32 [4096, 768], P(('dp', 'tensor'))
- x_grad: float32 [4096, 768], P(('dp', 'tensor'))
- ln1_gain_grad: float32 [1, 768], P(None, 'dp')
- ln1_bias_grad: float32 [1, 768], P(None, 'dp')
- ln2_gain_grad: float32 [1, 768], P(None, 'dp')
- ln2_bias_grad: float32 [1, 768], P(None, 'dp')
- qkv_weight_grad: float32 [1, 768, 2304], P(None, 'dp', 'tensor')
- qkv_bias_grad: float32 [1, 2304], P(None, 'tensor')
- dense_weight_grad: float32 [1, 768, 768], P(None, 'tensor', 'dp')
- dense_bias_grad: float32 [1, 768], P(None, 'dp')
- fc1_weight_grad: float32 [1, 768, 3072], P(None, 'dp', 'tensor')
- fc1_bias_grad: float32 [1, 3072], P(None, 'tensor')
- fc2_weight_grad: float32 [1, 3072, 768], P(None, 'tensor', 'dp')
- fc2_bias_grad: float32 [1, 768], P(None, 'dp')
The draws below stay inside these ranges and needn't reach their ends.
Inputs may be any that keep to these rules, and one draw needn't show every extreme that they name: `segments`: within each sequence of 512 tokens the segment numbers start at 0 and rise by one at each document's first token; every document has 60 to 800 tokens except the last of a sequence, which the sequence's end may cut. positions count 0, 1, 2, ... from each document's first token.
All inputs are finite; a program needn't handle non-finite values.
Results may differ from the reference program's by a relative error of at most 0.0055.
Values may be sent and summed in bfloat16 or wider, within the bound.
A program may use at most 128 MiB of HBM per device.

```python
import math
import jax
import jax.numpy as jnp
from jax import lax

D = 768
HEADS = 12
HEAD_DIM = 64
FF = 3072
ROT = 16
LAYERS = 1
SEQ = 512
DOC_LO = 60
DOC_HI = 800
TOKENS = 4096
N_DP = 8


def doc_layout(key):
    doc_slots = SEQ // DOC_LO + 1
    lengths = jax.random.randint(jax.random.fold_in(key, 11), (N_DP, doc_slots), DOC_LO, DOC_HI + 1)
    longest = min(DOC_HI, SEQ)
    lengths = lengths.at[N_DP - 1, :].set(DOC_LO)
    lengths = lengths.at[0, 0].set(longest)
    doc_ends = jnp.cumsum(lengths, axis=1)
    places = jnp.arange(SEQ, dtype=jnp.int32)
    passed = (places[None, :, None] >= doc_ends[:, None, :]).astype(jnp.int32)
    segment_ids = jnp.sum(passed, axis=2)
    starts = jnp.sum(passed * lengths[:, None, :], axis=2)
    offsets = places[None, :] - starts
    return (segment_ids.reshape(-1).astype(jnp.int32), offsets.reshape(-1).astype(jnp.int32))


def draw_segments(key, part):
    return doc_layout(key)[0]


def draw_positions(key, part):
    return doc_layout(key)[1]


def draw_qkv_weight(key, part):
    shape_full = (LAYERS, D, HEADS, 3, HEAD_DIM)
    spread = 0.5 / math.sqrt(D)
    base = jax.random.normal(key, shape_full, jnp.float32) * spread
    return base.reshape(LAYERS, D, 3 * D).astype(jnp.bfloat16)


def shard_levels(own_key, shape, pieces, low, top_value):
    factor_of = 1.0
    for position, shards_of in pieces:
        draws = jax.random.uniform(jax.random.fold_in(jax.random.fold_in(own_key, 6), position), (shards_of,), jnp.float32, low / len(pieces), top_value / len(pieces))
        factor_of = factor_of * jnp.repeat(jnp.exp(draws), shape[position] // shards_of).reshape((-1,) + (1,) * (len(shape) - 1 - position))
    return factor_of


def centred(rng, shape, scale, reach, split=(), held_as=jnp.bfloat16):
    entries = scale * jax.random.normal(rng, shape, jnp.float32)
    if split:
        entries = entries * shard_levels(rng, shape, split, -0.22, 0.18)
    return jnp.clip(entries, -reach, reach).astype(held_as)


def setup_inputs(seed: int = 0) -> dict:
    streams_of = jax.random.split(jax.random.key(seed), 17)
    return {
        "tokens": centred(streams_of[0], (TOKENS, D), 1.0, 6.0, ((0, 32),)),
        "segments": draw_segments(jax.random.fold_in(streams_of[16], 71), 0),
        "positions": draw_positions(jax.random.fold_in(streams_of[16], 71), 0),
        "ln1_gain": jnp.clip(1.0 + 0.1 * jax.random.normal(streams_of[3], (LAYERS, D), jnp.float32), 0.5, 1.5),
        "ln1_bias": centred(streams_of[4], (LAYERS, D), 0.3, 1.5, (), jnp.float32),
        "ln2_gain": jnp.clip(1.0 + 0.1 * jax.random.normal(streams_of[5], (LAYERS, D), jnp.float32), 0.5, 1.5),
        "ln2_bias": centred(streams_of[6], (LAYERS, D), 0.3, 1.5, (), jnp.float32),
        "qkv_weight": draw_qkv_weight(jax.random.fold_in(streams_of[16], 71), 0),
        "qkv_bias": centred(streams_of[8], (LAYERS, 3 * D), 0.3, 1.5, ((1, 4),), jnp.float32),
        "dense_weight": centred(streams_of[9], (LAYERS, D, D), (D // 16) ** -0.5, 0.875, ((1, 4), (2, 8))),
        "dense_bias": centred(streams_of[10], (LAYERS, D), 0.5, 2.5, (), jnp.float32),
        "fc1_weight": centred(streams_of[11], (LAYERS, D, FF), D ** -0.5, 0.21875, ((1, 8), (2, 4))),
        "fc1_bias": centred(streams_of[12], (LAYERS, FF), 0.5, 2.5, ((1, 4),), jnp.float32),
        "fc2_weight": centred(streams_of[13], (LAYERS, FF, D), FF ** -0.5, 0.109375, ((1, 4), (2, 8))),
        "fc2_bias": centred(streams_of[14], (LAYERS, D), 0.5, 2.5, (), jnp.float32),
        "cotangent": centred(streams_of[15], (TOKENS, D), 1.0, 6.0, ((0, 32),)),
    }


norm_eps = 1e-05

def rotary_tables(pos_ids):
    half_rot = ROT // 2
    inverse = 10000.0 ** (-(jnp.arange(half_rot, dtype=jnp.float32) * 2.0) / ROT)
    angles = pos_ids.astype(jnp.float32)[:, None] * inverse[None, :]
    cos_tab = jnp.concatenate([jnp.cos(angles), jnp.cos(angles)], axis=-1)
    sine_tab = jnp.concatenate([jnp.sin(angles), jnp.sin(angles)], axis=-1)
    return (cos_tab, sine_tab)

def rotate(blocked, cos_tab, sine_tab):
    head_part = blocked[..., :ROT]
    low_half = head_part[..., :ROT // 2]
    high_half = head_part[..., ROT // 2:]
    turned = jnp.concatenate([-high_half, low_half], axis=-1)
    spun_part = head_part * cos_tab[:, None, :] + turned * sine_tab[:, None, :]
    return jnp.concatenate([spun_part, blocked[..., ROT:]], axis=-1)

def unrotate(grad_part, cos_tab, sine_tab):
    head_part = grad_part[..., :ROT]
    scaled = head_part * sine_tab[:, None, :]
    back_turn = jnp.concatenate([scaled[..., ROT // 2:], -scaled[..., :ROT // 2]], axis=-1)
    return jnp.concatenate([head_part * cos_tab[:, None, :] + back_turn, grad_part[..., ROT:]], axis=-1)

def gelu_value(pre_act):
    return pre_act * 0.5 * (1.0 + jax.scipy.special.erf(pre_act / math.sqrt(2.0)))

def gelu_slope(pre_act):
    normal_cdf = 0.5 * (1.0 + jax.scipy.special.erf(pre_act / math.sqrt(2.0)))
    normal_pdf = jnp.exp(-0.5 * pre_act * pre_act) / math.sqrt(2.0 * math.pi)
    return normal_cdf + pre_act * normal_pdf

def block_mask(segment_ids, row_start, block_rows):
    seq_len = segment_ids.shape[0]
    columns = jnp.arange(seq_len, dtype=jnp.int32)
    row_ids = row_start + jnp.arange(block_rows, dtype=jnp.int32)
    seg_q = lax.dynamic_slice_in_dim(segment_ids, row_start, block_rows, 0)
    return (seg_q[:, None] == segment_ids[None, :]) & (row_ids[:, None] >= columns[None, :])

def attend(queries, key_rows, value_rows, segment_ids):
    seq_len = queries.shape[0]
    block_rows = min(512, seq_len)
    score_scale = HEAD_DIM ** (-0.5)
    keys_wide = key_rows.astype(jnp.float32)
    vals_wide = value_rows.astype(jnp.float32)

    def one_block(block_id):
        row_start = block_id * block_rows
        rows_q = lax.dynamic_slice_in_dim(queries, row_start, block_rows, 0).astype(jnp.float32)
        allowed = block_mask(segment_ids, row_start, block_rows)[None]
        scores = jnp.einsum('qhd,khd->hqk', rows_q, keys_wide) * score_scale
        scores = jnp.where(allowed, scores, -1e+30)
        row_max = lax.optimization_barrier(jnp.max(scores, axis=-1, keepdims=True))
        row_total = lax.optimization_barrier(jnp.sum(jnp.exp(scores - row_max), axis=-1, keepdims=True))
        log_total = row_max + jnp.log(row_total)
        attn_probs = jnp.where(allowed, jnp.exp(scores - log_total), 0.0).astype(jnp.bfloat16)
        context = jnp.einsum('hqk,khd->qhd', attn_probs.astype(jnp.float32), vals_wide)
        return (context, log_total[..., 0])
    contexts, totals = lax.map(one_block, jnp.arange(seq_len // block_rows, dtype=jnp.int32))
    context = contexts.reshape(seq_len, -1, HEAD_DIM)
    log_total = jnp.transpose(totals, (1, 0, 2)).reshape(totals.shape[1], seq_len)
    return (context, log_total)

def attend_back(queries, key_rows, value_rows, segment_ids, log_total, grad_ctx):
    seq_len = queries.shape[0]
    block_rows = min(512, seq_len)
    score_scale = HEAD_DIM ** (-0.5)
    keys_wide = key_rows.astype(jnp.float32)
    vals_wide = value_rows.astype(jnp.float32)
    zeros_kv = jnp.zeros(key_rows.shape, jnp.float32)

    def one_block(acc_pair, block_id):
        row_start = block_id * block_rows
        rows_q = lax.dynamic_slice_in_dim(queries, row_start, block_rows, 0).astype(jnp.float32)
        grad_blk = lax.dynamic_slice_in_dim(grad_ctx, row_start, block_rows, 0).astype(jnp.float32)
        lse_blk = lax.dynamic_slice_in_dim(log_total, row_start, block_rows, 1)
        allowed = block_mask(segment_ids, row_start, block_rows)[None]
        scores = jnp.einsum('qhd,khd->hqk', rows_q, keys_wide) * score_scale
        prob_wide = jnp.where(allowed, jnp.exp(scores - lse_blk[..., None]), 0.0)
        probs_bf = prob_wide.astype(jnp.bfloat16)
        grad_probs = jnp.einsum('qhd,khd->hqk', grad_blk, vals_wide)
        row_dot = lax.optimization_barrier(jnp.sum(prob_wide * grad_probs, axis=-1, keepdims=True))
        grad_scores = (prob_wide * (grad_probs - row_dot) * score_scale).astype(jnp.bfloat16).astype(jnp.float32)
        grad_q = jnp.einsum('hqk,khd->qhd', grad_scores, keys_wide)
        grad_keys = acc_pair[0] + jnp.einsum('hqk,qhd->khd', grad_scores, rows_q)
        grad_vals = acc_pair[1] + jnp.einsum('hqk,qhd->khd', probs_bf.astype(jnp.float32), grad_blk)
        return ((grad_keys, grad_vals), grad_q)
    (grad_keys, grad_vals), grad_qs = lax.scan(one_block, (zeros_kv, zeros_kv), jnp.arange(seq_len // block_rows, dtype=jnp.int32))
    return (grad_qs.reshape(seq_len, -1, HEAD_DIM), grad_keys, grad_vals)

def layer_forward(residual, params, segment_ids, cos_tab, sine_tab):
    gain_a, bias_a, gain_m, bias_m, w_qkv, b_qkv, w_dense, b_dense, w_up, b_up, w_down, b_down = params
    seq_len = residual.shape[0]
    center = residual - lax.optimization_barrier(jnp.mean(residual, axis=-1, keepdims=True))
    inv_std = lax.rsqrt(lax.optimization_barrier(jnp.mean(center * center, axis=-1, keepdims=True)) + norm_eps)
    normed = center * inv_std
    in_attn = (normed * gain_a + bias_a).astype(jnp.bfloat16)
    in_mlp = (normed * gain_m + bias_m).astype(jnp.bfloat16)
    joined_qkv = (jnp.dot(in_attn, w_qkv, preferred_element_type=jnp.float32) + b_qkv).reshape(seq_len, -1, 3, HEAD_DIM)
    queries = rotate(joined_qkv[:, :, 0], cos_tab, sine_tab).astype(jnp.bfloat16)
    key_rows = rotate(joined_qkv[:, :, 1], cos_tab, sine_tab).astype(jnp.bfloat16)
    value_rows = joined_qkv[:, :, 2].astype(jnp.bfloat16)
    context, log_total = attend(queries, key_rows, value_rows, segment_ids)
    context_bf = context.reshape(seq_len, -1).astype(jnp.bfloat16)
    pre_act = jnp.dot(in_mlp, w_up, preferred_element_type=jnp.float32) + b_up
    hidden = gelu_value(pre_act).astype(jnp.bfloat16)
    branch = jnp.dot(context_bf, w_dense, preferred_element_type=jnp.float32) + jnp.dot(hidden, w_down, preferred_element_type=jnp.float32)
    output_rows = residual + branch + b_dense + b_down
    saved = (normed, inv_std, in_attn, in_mlp, queries, key_rows, value_rows, log_total, context_bf, pre_act, hidden)
    return (output_rows, saved)

def layer_backward(grad_out, params, saved, segment_ids, cos_tab, sine_tab):
    gain_a, bias_a, gain_m, bias_m, w_qkv, b_qkv, w_dense, b_dense, w_up, b_up, w_down, b_down = params
    normed, inv_std, in_attn, in_mlp, queries, key_rows, value_rows, log_total, context_bf, pre_act, hidden = saved
    seq_len = grad_out.shape[0]
    grad_bf = grad_out.astype(jnp.bfloat16)
    grad_bias_out = lax.optimization_barrier(jnp.sum(grad_out, axis=0))
    grad_w_dense = jnp.dot(context_bf.T, grad_bf, preferred_element_type=jnp.float32)
    grad_w_down = jnp.dot(hidden.T, grad_bf, preferred_element_type=jnp.float32)
    grad_pre = jnp.dot(grad_bf, w_down.T, preferred_element_type=jnp.float32) * gelu_slope(pre_act)
    grad_b_up = lax.optimization_barrier(jnp.sum(grad_pre, axis=0))
    grad_pre_bf = grad_pre.astype(jnp.bfloat16)
    grad_ctx = jnp.dot(grad_bf, w_dense.T, preferred_element_type=jnp.float32).astype(jnp.bfloat16).reshape(seq_len, -1, HEAD_DIM)
    grad_w_up = jnp.dot(in_mlp.T, grad_pre_bf, preferred_element_type=jnp.float32)
    grad_in_mlp = jnp.dot(grad_pre_bf, w_up.T, preferred_element_type=jnp.float32)
    grad_q, grad_k, grad_v = attend_back(queries, key_rows, value_rows, segment_ids, log_total, grad_ctx)
    grad_joined = jnp.stack([unrotate(grad_q, cos_tab, sine_tab), unrotate(grad_k, cos_tab, sine_tab), grad_v], axis=2).reshape(seq_len, -1)
    grad_b_qkv = lax.optimization_barrier(jnp.sum(grad_joined, axis=0))
    grad_joined_bf = grad_joined.astype(jnp.bfloat16)
    grad_w_qkv = jnp.dot(in_attn.T, grad_joined_bf, preferred_element_type=jnp.float32)
    grad_in_attn = jnp.dot(grad_joined_bf, w_qkv.T, preferred_element_type=jnp.float32)
    grad_gain_a = lax.optimization_barrier(jnp.sum(grad_in_attn * normed, axis=0))
    grad_bias_a = lax.optimization_barrier(jnp.sum(grad_in_attn, axis=0))
    grad_gain_m = lax.optimization_barrier(jnp.sum(grad_in_mlp * normed, axis=0))
    grad_bias_m = lax.optimization_barrier(jnp.sum(grad_in_mlp, axis=0))
    grad_normed = grad_in_attn * gain_a + grad_in_mlp * gain_m
    grad_resid = inv_std * (grad_normed - lax.optimization_barrier(jnp.mean(grad_normed, axis=-1, keepdims=True)) - normed * lax.optimization_barrier(jnp.mean(grad_normed * normed, axis=-1, keepdims=True)))
    layer_grads = (grad_gain_a, grad_bias_a, grad_gain_m, grad_bias_m, grad_w_qkv, grad_b_qkv, grad_w_dense, grad_bias_out, grad_w_up, grad_b_up, grad_w_down)
    return (grad_out + grad_resid, layer_grads)

def reference(tokens, segments, positions, ln1_gain, ln1_bias, ln2_gain, ln2_bias, qkv_weight, qkv_bias, dense_weight, dense_bias, fc1_weight, fc1_bias, fc2_weight, fc2_bias, cotangent):
    params_all = (ln1_gain, ln1_bias, ln2_gain, ln2_bias, qkv_weight, qkv_bias, dense_weight, dense_bias, fc1_weight, fc1_bias, fc2_weight, fc2_bias)
    grad_init = tuple((jnp.zeros(member.shape, jnp.float32) for member in params_all[:11]))
    seq_tokens = tokens.reshape(N_DP, SEQ, D)
    seq_cots = cotangent.reshape(N_DP, SEQ, D)
    seq_segs = segments.reshape(N_DP, SEQ)
    seq_poss = positions.reshape(N_DP, SEQ)

    def one_sequence(totals, inputs_seq):
        seq_rows, seq_cot, seg_ids, pos_ids = inputs_seq
        cos_tab, sine_tab = rotary_tables(pos_ids)
        residual = seq_rows.astype(jnp.float32)
        kept_all = []
        for layer_id in range(LAYERS):
            params = tuple((member[layer_id] for member in params_all))
            residual, saved = layer_forward(residual, params, seg_ids, cos_tab, sine_tab)
            kept_all.append(saved)
        grad_flow = seq_cot.astype(jnp.float32)
        for layer_id in reversed(range(LAYERS)):
            params = tuple((member[layer_id] for member in params_all))
            grad_flow, layer_grads = layer_backward(grad_flow, params, kept_all[layer_id], seg_ids, cos_tab, sine_tab)
            totals = tuple((total_arr.at[layer_id].add(grad_arr) for total_arr, grad_arr in zip(totals, layer_grads)))
        return (totals, (residual, grad_flow))
    totals, (outputs_seq, grads_seq) = lax.scan(one_sequence, grad_init, (seq_tokens, seq_cots, seq_segs, seq_poss))
    return (outputs_seq.reshape(-1, D), grads_seq.reshape(-1, D), totals[0], totals[1], totals[2], totals[3], totals[4], totals[5], totals[6], totals[7], totals[8], totals[9], totals[10], totals[7])
```

```python
import math

import jax
import jax.numpy as jnp
from jax import lax
from jax.experimental import pallas as pl
from jax.experimental.pallas import tpu as pltpu
from jax.sharding import PartitionSpec as P

HEAD_DIM = 64
ROT = 16
PAIR = 2
MESH = pl.DeviceIdType.MESH

norm_eps = 1e-05


def places(n_dp, n_t):
    dp = lax.axis_index("dp")
    t = lax.axis_index("tensor")
    return dp, t, dp // PAIR, lax.rem(dp, PAIR), n_dp // PAIR


def greet(devices):
    barrier = pltpu.get_barrier_semaphore()
    for device, there in devices:
        if there is None:
            pl.semaphore_signal(barrier, inc=1, device_id=device, device_id_type=MESH)
        else:

            @pl.when(there)
            def _(device=device):
                pl.semaphore_signal(barrier, inc=1, device_id=device, device_id_type=MESH)

    expected = sum(1 if there is None else there.astype(jnp.int32) for _, there in devices)
    pl.semaphore_wait(barrier, expected)


def gather_kernel(n_dp, n_t, n_w, *refs):
    w_in = refs[:n_w]
    rows_in = refs[n_w : n_w + 2]
    w_out = refs[n_w + 2 : 2 * n_w + 2]
    rows_out = refs[2 * n_w + 2 : 2 * n_w + 4]
    r_send, r_recv, l_send, l_recv, y_send, y_recv, t_send, t_recv = refs[2 * n_w + 4 :]
    dp, t, z, y, height = places(n_dp, n_t)
    mate = (z * PAIR + (1 - y), t)
    right = (jnp.minimum(z + 1, height - 1) * PAIR + y, t)
    left = (jnp.maximum(z - 1, 0) * PAIR + y, t)
    has_right = z + 1 < height
    has_left = z >= 1
    greet(
        [(mate, None), (right, has_right), (left, has_left)]
        + [((dp, lax.rem(t + k, n_t)), None) for k in range(1, n_t)]
    )

    def line(src, a, block, step, send, recv, device):
        return pltpu.make_async_remote_copy(
            src_ref=src,
            dst_ref=w_out[a].at[block * PAIR + y],
            send_sem=send.at[a, step],
            recv_sem=recv.at[a, step],
            device_id=device,
            device_id_type=MESH,
        )

    def across(src, a, block, side):
        return pltpu.make_async_remote_copy(
            src_ref=src,
            dst_ref=w_out[a].at[block * PAIR + side],
            send_sem=y_send.at[a, block],
            recv_sem=y_recv.at[a, block],
            device_id=mate,
            device_id_type=MESH,
        )

    def peer_copy(i, k, owner):
        return pltpu.make_async_remote_copy(
            src_ref=rows_in[i],
            dst_ref=rows_out[i].at[owner],
            send_sem=t_send.at[i, k - 1],
            recv_sem=t_recv.at[i, k - 1],
            device_id=(dp, lax.rem(t + k, n_t)),
            device_id_type=MESH,
        )

    for a in range(n_w):

        @pl.when(has_right)
        def _(a=a):
            line(w_in[a], a, z, 0, r_send, r_recv, right).start()

        @pl.when(has_left)
        def _(a=a):
            line(w_in[a], a, z, 0, l_send, l_recv, left).start()

        across(w_in[a], a, z, y).start()
    for i in range(2):
        for k in range(1, n_t):
            peer_copy(i, k, t).start()
    for a in range(n_w):
        w_out[a][dp] = w_in[a][...]
    for i in range(2):
        rows_out[i][t] = rows_in[i][...]

    for step in range(height - 1):
        for a in range(n_w):
            from_left = z - 1 - step
            from_right = z + 1 + step

            @pl.when(from_left >= 0)
            def _(a=a, block=from_left, step=step):
                held = w_out[a].at[block * PAIR + y]
                line(held, a, block, step, r_send, r_recv, right).wait_recv()
                across(held, a, block, y).start()
                if step + 1 < height - 1:

                    @pl.when(has_right)
                    def _():
                        line(held, a, block, step + 1, r_send, r_recv, right).start()

            @pl.when(from_right < height)
            def _(a=a, block=from_right, step=step):
                held = w_out[a].at[block * PAIR + y]
                line(held, a, block, step, l_send, l_recv, left).wait_recv()
                across(held, a, block, y).start()
                if step + 1 < height - 1:

                    @pl.when(has_left)
                    def _():
                        line(held, a, block, step + 1, l_send, l_recv, left).start()

    for i in range(2):
        for k in range(1, n_t):
            peer_copy(i, k, lax.rem(t + n_t - k, n_t)).wait_recv()
            peer_copy(i, k, t).wait_send()
    for a in range(n_w):
        for step in range(height - 1):

            @pl.when((z - step >= 0) & has_right)
            def _(a=a, step=step):
                line(w_in[a], a, z, step, r_send, r_recv, right).wait_send()

            @pl.when((z + step < height) & has_left)
            def _(a=a, step=step):
                line(w_in[a], a, z, step, l_send, l_recv, left).wait_send()

        for block in range(height):
            across(w_in[a], a, block, y).wait_send()
            across(w_in[a], a, block, 1 - y).wait_recv()


def gather_all(weights, rows, n_dp, n_t):
    n_w = len(weights)
    height = n_dp // PAIR
    vmem = pl.BlockSpec(memory_space=pltpu.VMEM)
    dma = pltpu.SemaphoreType.DMA

    def kernel(*refs):
        gather_kernel(n_dp, n_t, n_w, *refs)

    return pl.pallas_call(
        kernel,
        out_shape=[jax.ShapeDtypeStruct((n_dp,) + w.shape, w.dtype) for w in weights]
        + [jax.ShapeDtypeStruct((n_t,) + r.shape, r.dtype) for r in rows],
        in_specs=[vmem] * (n_w + 2),
        out_specs=[vmem] * (n_w + 2),
        scratch_shapes=[
            dma((n_w, height - 1)),
            dma((n_w, height - 1)),
            dma((n_w, height - 1)),
            dma((n_w, height - 1)),
            dma((n_w, height)),
            dma((n_w, height)),
            dma((2, n_t - 1)),
            dma((2, n_t - 1)),
        ],
        compiler_params=pltpu.CompilerParams(collective_id=0, has_side_effects=True),
        name="gather_all",
    )(*weights, *rows)


def reduce_kernel(n_dp, n_t, n_w, n_r, *refs):
    g_in = refs[:n_w]
    p_in = refs[n_w : n_w + n_r]
    vec_in = refs[n_w + n_r]
    base = n_w + n_r + 1
    g_out = refs[base : base + n_w]
    p_out = refs[base + n_w : base + n_w + n_r]
    vec_out = refs[base + n_w + n_r]
    base = 2 * base
    y_buf = refs[base : base + n_w]
    s_buf = refs[base + n_w : base + 2 * n_w]
    z_buf = refs[base + 2 * n_w : base + 3 * n_w]
    base += 3 * n_w
    p_buf = refs[base : base + n_r]
    vy_buf, vs_buf, vz_buf, vd_buf, vt_buf = refs[base + n_r : base + n_r + 5]
    (
        y_send,
        y_recv,
        z_send,
        z_recv,
        p_send,
        p_recv,
        v_send,
        v_recv,
    ) = refs[base + n_r + 5 :]
    dp, t, z, y, height = places(n_dp, n_t)
    mate = (z * PAIR + (1 - y), t)

    def at_z(k):
        return lax.rem(z + k, height)

    greet(
        [(mate, None)]
        + [((at_z(k) * PAIR + y, t), None) for k in range(1, height)]
        + [((dp, lax.rem(t + k, n_t)), None) for k in range(1, n_t)]
    )

    def remote(src, dst, send, recv, device):
        return pltpu.make_async_remote_copy(
            src_ref=src,
            dst_ref=dst,
            send_sem=send,
            recv_sem=recv,
            device_id=device,
            device_id_type=MESH,
        )

    order = [k for k in range(1, height)] + [0]

    def swap(a, k):
        return remote(
            g_in[a].at[at_z(k) * PAIR + (1 - y)],
            y_buf[a].at[k],
            y_send.at[a, k],
            y_recv.at[a, k],
            mate,
        )

    def to_owner(a, k):
        return remote(
            s_buf[a].at[k - 1],
            z_buf[a].at[k - 1],
            z_send.at[a, k - 1],
            z_recv.at[a, k - 1],
            (at_z(k) * PAIR + y, t),
        )

    def to_peer(i, k):
        return remote(
            p_in[i].at[lax.rem(t + k, n_t)],
            p_buf[i].at[k - 1],
            p_send.at[i, k - 1],
            p_recv.at[i, k - 1],
            (dp, lax.rem(t + k, n_t)),
        )

    vec_swap = remote(vec_in, vy_buf, v_send.at[0], v_recv.at[0], mate)

    def vec_owner(k):
        return remote(
            vs_buf, vz_buf.at[k - 1], v_send.at[k], v_recv.at[k], (at_z(k) * PAIR + y, t)
        )

    def vec_peer(k):
        at = height - 1 + k
        return remote(
            vd_buf, vt_buf.at[k - 1], v_send.at[at], v_recv.at[at], (dp, lax.rem(t + k, n_t))
        )

    vec_swap.start()
    for k in order:
        for a in range(n_w):
            swap(a, k).start()
    for i in range(n_r):
        for k in range(1, n_t):
            to_peer(i, k).start()

    vec_swap.wait_recv()
    vs_buf[...] = vec_in[...] + vy_buf[...]
    for k in range(1, height):
        vec_owner(k).start()

    for k in range(1, height):
        for a in range(n_w):
            swap(a, k).wait_recv()
            own = g_in[a][at_z(k) * PAIR + y].astype(jnp.float32)
            s_buf[a][k - 1] = (own + y_buf[a][k].astype(jnp.float32)).astype(jnp.bfloat16)
            to_owner(a, k).start()
        if k == 1:
            total = vs_buf[...]
            for j in range(1, height):
                vec_owner(j).wait_recv()
                total = total + vz_buf[j - 1]
            vd_buf[...] = total
            for j in range(1, n_t):
                vec_peer(j).start()

    for i in range(n_r):
        total = p_in[i][t].astype(jnp.float32)
        for k in range(1, n_t):
            to_peer(i, k).wait_recv()
            total = total + p_buf[i][k - 1].astype(jnp.float32)
        p_out[i][...] = total

    total = vd_buf[...]
    for k in range(1, n_t):
        vec_peer(k).wait_recv()
        total = total + vt_buf[k - 1]
    vec_out[0] = vd_buf[...]
    vec_out[1] = total

    for a in range(n_w):
        swap(a, 0).wait_recv()
        total = g_in[a][dp].astype(jnp.float32) + y_buf[a][0].astype(jnp.float32)
        g_out[a][...] = total
    for k in range(1, height):
        for a in range(n_w):
            to_owner(a, k).wait_recv()
            g_out[a][...] += z_buf[a][k - 1].astype(jnp.float32)

    vec_swap.wait_send()
    for k in range(1, height):
        vec_owner(k).wait_send()
    for k in range(1, n_t):
        vec_peer(k).wait_send()
    for a in range(n_w):
        for k in range(height):
            swap(a, k).wait_send()
        for k in range(1, height):
            to_owner(a, k).wait_send()
    for i in range(n_r):
        for k in range(1, n_t):
            to_peer(i, k).wait_send()


def reduce_all(grads, parts, vec, n_dp, n_t):
    n_w, n_r = len(grads), len(parts)
    height = n_dp // PAIR
    vmem = pl.BlockSpec(memory_space=pltpu.VMEM)
    dma = pltpu.SemaphoreType.DMA

    def kernel(*refs):
        reduce_kernel(n_dp, n_t, n_w, n_r, *refs)

    n_in = n_w + n_r + 1
    n_vec = height + n_t - 1
    return pl.pallas_call(
        kernel,
        out_shape=[jax.ShapeDtypeStruct(g.shape[1:], jnp.float32) for g in grads]
        + [jax.ShapeDtypeStruct(p.shape[1:], jnp.float32) for p in parts]
        + [jax.ShapeDtypeStruct((2,) + vec.shape, jnp.float32)],
        in_specs=[vmem] * n_in,
        out_specs=[vmem] * n_in,
        scratch_shapes=[pltpu.VMEM((height,) + g.shape[1:], jnp.bfloat16) for g in grads]
        + [pltpu.VMEM((height - 1,) + g.shape[1:], jnp.bfloat16) for g in grads]
        + [pltpu.VMEM((height - 1,) + g.shape[1:], jnp.bfloat16) for g in grads]
        + [pltpu.VMEM((n_t - 1,) + p.shape[1:], jnp.bfloat16) for p in parts]
        + [
            pltpu.VMEM(vec.shape, jnp.float32),
            pltpu.VMEM(vec.shape, jnp.float32),
            pltpu.VMEM((height - 1,) + vec.shape, jnp.float32),
            pltpu.VMEM(vec.shape, jnp.float32),
            pltpu.VMEM((n_t - 1,) + vec.shape, jnp.float32),
        ]
        + [
            dma((n_w, height)),
            dma((n_w, height)),
            dma((n_w, height - 1)),
            dma((n_w, height - 1)),
            dma((n_r, n_t - 1)),
            dma((n_r, n_t - 1)),
            dma((n_vec,)),
            dma((n_vec,)),
        ],
        compiler_params=pltpu.CompilerParams(collective_id=1, has_side_effects=True),
        name="reduce_all",
    )(*grads, *parts, vec)


def dot(left, right, dims):
    return lax.dot_general(left, right, (dims, ((), ())), preferred_element_type=jnp.float32)


NN = ((1,), (0,))
NT = ((1,), (1,))
TN = ((0,), (0,))


def fused_kernel(n_dp, n_t, refs):
    bf16, f32 = jnp.bfloat16, jnp.float32
    n_w = 4
    (
        w_up_in,
        w_down_in,
        w_qkv_in,
        w_dense_in,
        tok_in,
        cot_in,
        gain_a,
        bias_a,
        gain_m,
        bias_m,
        b_qkv,
        b_up,
        b_dense,
        b_down,
        seg_row,
        pos_row,
        y_ref,
        x_ref,
        g_up,
        g_down,
        g_qkv,
        g_dense,
        vec_out,
        qkv_bias_out,
        up_bias_out,
    ) = refs[:25]
    rest = list(refs[25:])

    def take(n):
        got = rest[:n]
        del rest[:n]
        return got

    w_all, g_in, y_buf, s_buf, z_buf = take(4), take(4), take(4), take(4), take(4)
    rows_all, p_in, p_buf, p_sum = take(2), take(3), take(3), take(3)
    vec_in, vy_buf, vs_buf, vz_buf, vd_buf, vt_buf = take(6)
    normed, in_a, in_m, in_at, in_mt, grad_t, hidden, grad_pre, joined, cos_w, sin_a, sin_b = take(12)
    w_dense_t, g_dense_t = take(2)
    r_send, r_recv, l_send, l_recv, f_send, f_recv, t_send, t_recv = take(8)
    y_send, y_recv, z_send, z_recv, p_send, p_recv, v_send, v_recv = take(8)
    w_in = (w_up_in, w_down_in, w_qkv_in, w_dense_t)
    g_out = (g_up, g_down, g_qkv, g_dense_t)

    dp, t, z, y, height = places(n_dp, n_t)
    group, width = tok_in.shape
    seq = group * n_t
    wide = joined.shape[1]
    heads_wide = w_qkv_in.shape[1]
    n_heads = heads_wide // (3 * HEAD_DIM)
    mate = (z * PAIR + (1 - y), t)
    right = (jnp.minimum(z + 1, height - 1) * PAIR + y, t)
    left = (jnp.maximum(z - 1, 0) * PAIR + y, t)
    has_right = z + 1 < height
    has_left = z >= 1

    def at_z(k):
        return lax.rem(z + k, height)

    def z_device(k):
        return (at_z(k) * PAIR + y, t)

    def t_device(k):
        return (dp, lax.rem(t + k, n_t))

    greet(
        [(mate, None)]
        + [(z_device(k), None) for k in range(1, height)]
        + [(t_device(k), None) for k in range(1, n_t)]
    )

    def remote(src, dst, send, recv, device):
        return pltpu.make_async_remote_copy(
            src_ref=src,
            dst_ref=dst,
            send_sem=send,
            recv_sem=recv,
            device_id=device,
            device_id_type=MESH,
        )

    def line(src, a, block, step, send, recv, device):
        return remote(
            src, w_all[a].at[block * PAIR + y], send.at[a, step], recv.at[a, step], device
        )

    def across(src, a, block, side):
        return remote(
            src, w_all[a].at[block * PAIR + side], f_send.at[a, block], f_recv.at[a, block], mate
        )

    rows_in = (tok_in, cot_in)

    def peer_copy(i, k, owner):
        return remote(
            rows_in[i], rows_all[i].at[owner], t_send.at[i, k - 1], t_recv.at[i, k - 1], t_device(k)
        )

    def swap(a, k):
        return remote(
            g_in[a].at[at_z(k) * PAIR + (1 - y)],
            y_buf[a].at[k],
            y_send.at[a, k],
            y_recv.at[a, k],
            mate,
        )

    def to_owner(a, k):
        return remote(
            s_buf[a].at[k - 1],
            z_buf[a].at[k - 1],
            z_send.at[a, k - 1],
            z_recv.at[a, k - 1],
            z_device(k),
        )

    def to_peer(i, k):
        return remote(
            p_in[i].at[lax.rem(t + k, n_t)],
            p_buf[i].at[k - 1],
            p_send.at[i, k - 1],
            p_recv.at[i, k - 1],
            t_device(k),
        )

    vec_swap = remote(vec_in, vy_buf, v_send.at[0], v_recv.at[0], mate)

    def vec_owner(k):
        return remote(vs_buf, vz_buf.at[k - 1], v_send.at[k], v_recv.at[k], z_device(k))

    def vec_peer(k):
        at = height - 1 + k
        return remote(vd_buf, vt_buf.at[k - 1], v_send.at[at], v_recv.at[at], t_device(k))

    for a in range(n_w):
        if a == 3:
            w_dense_t[...] = w_dense_in[...].T

        @pl.when(has_right)
        def _(a=a):
            line(w_in[a], a, z, 0, r_send, r_recv, right).start()

        @pl.when(has_left)
        def _(a=a):
            line(w_in[a], a, z, 0, l_send, l_recv, left).start()

        across(w_in[a], a, z, y).start()
        if a == 0:
            for i in range(2):
                for k in range(1, n_t):
                    peer_copy(i, k, t).start()
    for a in range(n_w):
        w_all[a][dp] = w_in[a][...]
    for i in range(2):
        rows_all[i][t] = rows_in[i][...]

    def relay(step, arrays):
        for a in arrays:
            from_left = z - 1 - step
            from_right = z + 1 + step

            @pl.when(from_left >= 0)
            def _(a=a, block=from_left):
                held = w_all[a].at[block * PAIR + y]
                line(held, a, block, step, r_send, r_recv, right).wait_recv()
                across(held, a, block, y).start()
                if step + 1 < height - 1:

                    @pl.when(has_right)
                    def _():
                        line(held, a, block, step + 1, r_send, r_recv, right).start()

            @pl.when(from_right < height)
            def _(a=a, block=from_right):
                held = w_all[a].at[block * PAIR + y]
                line(held, a, block, step, l_send, l_recv, left).wait_recv()
                across(held, a, block, y).start()
                if step + 1 < height - 1:

                    @pl.when(has_left)
                    def _():
                        line(held, a, block, step + 1, l_send, l_recv, left).start()

    def land(arrays):
        for a in arrays:
            for block in range(height):
                across(w_in[a], a, block, 1 - y).wait_recv()

    lanes = lax.broadcasted_iota(jnp.int32, (8, wide), 1)
    subs = lax.broadcasted_iota(jnp.int32, (8, wide), 0)
    part = lax.rem(lanes, HEAD_DIM)
    kind = lax.rem(lanes // HEAD_DIM, 3)
    turning = (kind < 2) & (lanes < heads_wide)
    low = (turning & (part == subs)).astype(f32)
    high = (turning & (part == subs + ROT // 2)).astype(f32)
    still = 1.0 - jnp.sum(low + high, axis=0, keepdims=True)

    def spread(table, where):
        return lax.dot_general(
            table, where, (TN, ((), ())), preferred_element_type=f32, precision=lax.Precision.HIGHEST
        )

    half_rot = ROT // 2
    order = lax.broadcasted_iota(jnp.int32, (half_rot, seq), 0)
    inverse = jnp.zeros((half_rot, seq), f32)
    for i in range(half_rot):
        inverse = jnp.where(order == i, 10000.0 ** (-2.0 * i / ROT), inverse)
    angles = pos_row[...].astype(f32) * inverse
    cos8, sin8 = jnp.cos(angles), jnp.sin(angles)
    cos_w[...] = spread(cos8, low + high) + still
    sin_a[...] = -spread(sin8, low)
    sin_b[...] = spread(sin8, high)

    relay(0, (0, 1))
    for i in range(2):
        for k in range(1, n_t):
            peer_copy(i, k, lax.rem(t + n_t - k, n_t)).wait_recv()

    def norm_of(rows):
        center = rows - jnp.mean(rows, axis=-1, keepdims=True)
        inv_std = lax.rsqrt(jnp.mean(center * center, axis=-1, keepdims=True) + norm_eps)
        return center * inv_std, inv_std

    for g in range(n_t):
        at = pl.ds(g * group, group)
        value, _ = norm_of(rows_all[0][g].astype(f32))
        normed[at, :] = value
        va = (value * gain_a[...] + bias_a[...]).astype(bf16)
        vm = (value * gain_m[...] + bias_m[...]).astype(bf16)
        in_a[at, :] = va
        in_m[at, :] = vm
        in_at[:, at] = va.T
        in_mt[:, at] = vm.T
        grad_t[:, at] = rows_all[1][g].T
    relay(1, (0, 1))
    grad_full = rows_all[1][...].reshape(seq, width)
    for step in range(2, height - 1):
        relay(step, (0, 1))
    relay(0, (2, 3))
    land((0, 1))

    w_up = w_all[0][...].reshape(width, -1)
    w_down = w_all[1][...].reshape(width, -1)

    vec_in[...] = jnp.zeros_like(vec_in)
    for g in range(n_t):
        at = pl.ds(g * group, group)
        pre = dot(in_m[at, :], w_up, NN) + b_up[...]
        cdf = 0.5 * (1.0 + lax.erf(pre / math.sqrt(2.0)))
        pdf = jnp.exp(-0.5 * pre * pre) / math.sqrt(2.0 * math.pi)
        hidden[at, :] = (pre * cdf).astype(bf16)
        gp = dot(rows_all[1][g], w_down, NN) * (cdf + pre * pdf)
        vec_in[6:7, : gp.shape[1]] += jnp.sum(gp, axis=0, keepdims=True)
        grad_pre[at, :] = gp.astype(bf16)
        if g == 1:
            for step in range(1, height - 1):
                relay(step, (2, 3))

    def blocks(grad, share):
        return grad.astype(bf16).reshape(n_dp, width // n_dp, share)

    g_in[0][...] = blocks(dot(in_mt[...], grad_pre[...], NN), w_up.shape[1])
    for k in list(range(1, height)) + [0]:
        swap(0, k).start()
    g_in[1][...] = blocks(dot(grad_t[...], hidden[...], NN), w_down.shape[1])
    for k in list(range(1, height)) + [0]:
        swap(1, k).start()
    for g in range(n_t):
        at = pl.ds(g * group, group)
        pm = dot(grad_pre[at, :], w_up, NT)
        vec_in[2:3, :width] += jnp.sum(pm * normed[at, :], axis=0, keepdims=True)
        vec_in[3:4, :width] += jnp.sum(pm, axis=0, keepdims=True)
        p_in[2][g] = pm.astype(bf16)
    for k in range(1, n_t):
        to_peer(2, k).start()

    def settle(k, arrays):
        for a in arrays:
            swap(a, k).wait_recv()
            own = g_in[a][at_z(k) * PAIR + y].astype(f32)
            s_buf[a][k - 1] = (own + y_buf[a][k].astype(f32)).astype(bf16)
            to_owner(a, k).start()

    land((2, 3))
    w_qkv = w_all[2][...].reshape(width, -1)
    w_dense = w_all[3][...].reshape(width, -1)
    joined[...] = jnp.zeros_like(joined)
    joined[:, :heads_wide] = dot(in_a[...], w_qkv, NN) + b_qkv[...]

    def turn(value, sign):
        moved = pltpu.roll(value, wide - ROT // 2, 1) * sin_a[...]
        moved = moved + pltpu.roll(value, ROT // 2, 1) * sin_b[...]
        return value * cos_w[...] + sign * moved

    turned = turn(joined[...], 1.0).astype(bf16)
    grad_ctx = dot(grad_full, w_dense, NN).astype(bf16)
    row_at = lax.broadcasted_iota(jnp.int32, (seq, seq), 0)
    col_at = lax.broadcasted_iota(jnp.int32, (seq, seq), 1)
    seg_at = seg_row[...].astype(f32)
    seg_col = jnp.broadcast_to(seg_at, (128, seq)).T[:, :1]
    allowed = (seg_col == seg_at) & (row_at >= col_at)
    scale = HEAD_DIM ** (-0.5)
    contexts = []
    for h in range(n_heads):
        base = h * 3 * HEAD_DIM
        q = turned[:, base : base + HEAD_DIM]
        k_h = turned[:, base + HEAD_DIM : base + 2 * HEAD_DIM]
        v = turned[:, base + 2 * HEAD_DIM : base + 3 * HEAD_DIM]
        gc = grad_ctx[:, h * HEAD_DIM : (h + 1) * HEAD_DIM]
        scores = jnp.where(allowed, dot(q, k_h, NT) * scale, -1e30)
        e = jnp.exp(scores - jnp.max(scores, axis=-1, keepdims=True))
        p = e * (1.0 / jnp.sum(e, axis=-1, keepdims=True))
        pb = p.astype(bf16)
        contexts.append(dot(pb, v, NN).astype(bf16))
        gp = dot(gc, v, NT)
        row_dot = jnp.sum(p * gp, axis=-1, keepdims=True)
        gs = (p * (gp - row_dot) * scale).astype(bf16)
        joined[:, base : base + HEAD_DIM] = dot(gs, k_h, NN)
        joined[:, base + HEAD_DIM : base + 2 * HEAD_DIM] = dot(gs, q, TN)
        joined[:, base + 2 * HEAD_DIM : base + 3 * HEAD_DIM] = dot(pb, gc, TN)
        for k in range(1, height):
            if min(k, n_heads) - 1 == h:
                settle(k, (0, 1))
    context = jnp.concatenate(contexts, axis=1)
    grad_joined = turn(joined[...], -1.0)[:, :heads_wide]
    vec_in[5:6, :heads_wide] = jnp.sum(grad_joined, axis=0, keepdims=True)
    gj = grad_joined.astype(bf16)
    g_in[2][...] = blocks(dot(in_at[...], gj, NN), heads_wide)
    for k in list(range(1, height)) + [0]:
        swap(2, k).start()
    g_in[3][...] = blocks(dot(grad_t[...], context, NN), w_dense.shape[1])
    for k in list(range(1, height)) + [0]:
        swap(3, k).start()
    for g in range(n_t):
        at = pl.ds(g * group, group)
        pa = dot(gj[g * group : (g + 1) * group], w_qkv, NT)
        vec_in[0:1, :width] += jnp.sum(pa * normed[at, :], axis=0, keepdims=True)
        vec_in[1:2, :width] += jnp.sum(pa, axis=0, keepdims=True)
        p_in[1][g] = pa.astype(bf16)
    grad_rows = cot_in[...].astype(f32)
    vec_in[4:5, :width] = jnp.sum(grad_rows, axis=0, keepdims=True)
    vec_swap.start()
    for k in range(1, n_t):
        to_peer(1, k).start()
    for g in range(n_t):
        at = pl.ds(g * group, group)
        branch = dot(context[g * group : (g + 1) * group], w_dense, NT)
        p_in[0][g] = (branch + dot(hidden[at, :], w_down, NT)).astype(bf16)
    for k in range(1, n_t):
        to_peer(0, k).start()
    for k in range(1, height):
        settle(k, (2, 3))
        if k == 1:
            vec_swap.wait_recv()
            vs_buf[...] = vec_in[...] + vy_buf[...]
            for j in range(1, height):
                vec_owner(j).start()

    def finish(arrays):
        for a in arrays:
            swap(a, 0).wait_recv()
            total = g_in[a][dp].astype(f32) + y_buf[a][0].astype(f32)
            for k in range(1, height):
                to_owner(a, k).wait_recv()
                total = total + z_buf[a][k - 1].astype(f32)
            g_out[a][...] = total

    finish((0, 1))
    total = vs_buf[...]
    for j in range(1, height):
        vec_owner(j).wait_recv()
        total = total + vz_buf[j - 1]
    vd_buf[...] = total
    for j in range(1, n_t):
        vec_peer(j).start()

    for i in range(3):
        total = p_in[i][t].astype(f32)
        for k in range(1, n_t):
            to_peer(i, k).wait_recv()
            total = total + p_buf[i][k - 1].astype(f32)
        p_sum[i][...] = total
    own = tok_in[...].astype(f32)
    own_normed, inv_std = norm_of(own)
    y_ref[...] = own + p_sum[0][...] + b_dense[...] + b_down[...]
    grad_normed = p_sum[1][...] * gain_a[...] + p_sum[2][...] * gain_m[...]
    x_ref[...] = grad_rows + inv_std * (
        grad_normed
        - jnp.mean(grad_normed, axis=-1, keepdims=True)
        - own_normed * jnp.mean(grad_normed * own_normed, axis=-1, keepdims=True)
    )
    total = vd_buf[...]
    for k in range(1, n_t):
        vec_peer(k).wait_recv()
        total = total + vt_buf[k - 1]
    share = w_up_in.shape[0]
    owned = jnp.zeros((8, share), f32)
    for d in range(n_dp):
        owned = jnp.where(dp == d, total[:, d * share : (d + 1) * share], owned)
    vec_out[...] = owned
    qkv_bias_out[...] = vd_buf[5:6, :heads_wide]
    up_bias_out[...] = vd_buf[6:7, : w_up_in.shape[1]]
    finish((2, 3))
    g_dense[...] = g_dense_t[...].T

    for i in range(2):
        for k in range(1, n_t):
            peer_copy(i, k, t).wait_send()
    for a in range(n_w):
        for step in range(height - 1):

            @pl.when((z - step >= 0) & has_right)
            def _(a=a, step=step):
                line(w_in[a], a, z, step, r_send, r_recv, right).wait_send()

            @pl.when((z + step < height) & has_left)
            def _(a=a, step=step):
                line(w_in[a], a, z, step, l_send, l_recv, left).wait_send()

        for block in range(height):
            across(w_in[a], a, block, y).wait_send()
        for k in range(height):
            swap(a, k).wait_send()
        for k in range(1, height):
            to_owner(a, k).wait_send()
    vec_swap.wait_send()
    for k in range(1, height):
        vec_owner(k).wait_send()
    for k in range(1, n_t):
        vec_peer(k).wait_send()
        for i in range(3):
            to_peer(i, k).wait_send()


def fused_layer(weights, rows, vectors, tables, n_dp, n_t):
    height = n_dp // PAIR
    bf16, f32 = jnp.bfloat16, jnp.float32
    group, width = rows[0].shape
    seq = group * n_t
    heads_wide = weights[2].shape[1]
    wide = -(-heads_wide // 128) * 128
    units = weights[0].shape[1]
    n_vec = max(width, heads_wide, units)
    vmem = pl.BlockSpec(memory_space=pltpu.VMEM)
    dma = pltpu.SemaphoreType.DMA
    n_vs = height + n_t - 1
    shapes = [w.shape for w in weights[:3]] + [weights[3].shape[::-1]]

    def buf(*shape, dtype=bf16):
        return pltpu.VMEM(shape, dtype)

    def per_weight(lead):
        return [buf(lead, *s) for s in shapes]

    def kernel(*refs):
        fused_kernel(n_dp, n_t, refs)

    return pl.pallas_call(
        kernel,
        out_shape=[jax.ShapeDtypeStruct((group, width), f32)] * 2
        + [jax.ShapeDtypeStruct(w.shape, f32) for w in weights]
        + [
            jax.ShapeDtypeStruct((8, width // n_dp), f32),
            jax.ShapeDtypeStruct((1, heads_wide), f32),
            jax.ShapeDtypeStruct((1, units), f32),
        ],
        in_specs=[vmem] * 16,
        out_specs=[vmem] * 9,
        scratch_shapes=per_weight(n_dp)
        + per_weight(n_dp)
        + per_weight(height)
        + per_weight(height - 1)
        + per_weight(height - 1)
        + [buf(n_t, group, width)] * 2
        + [buf(n_t, group, width)] * 3
        + [buf(n_t - 1, group, width)] * 3
        + [buf(group, width, dtype=f32)] * 3
        + [
            buf(8, n_vec, dtype=f32),
            buf(8, n_vec, dtype=f32),
            buf(8, n_vec, dtype=f32),
            buf(height - 1, 8, n_vec, dtype=f32),
            buf(8, n_vec, dtype=f32),
            buf(n_t - 1, 8, n_vec, dtype=f32),
            buf(seq, width, dtype=f32),
            buf(seq, width),
            buf(seq, width),
            buf(width, seq),
            buf(width, seq),
            buf(width, seq),
            buf(seq, units),
            buf(seq, units),
            buf(seq, wide, dtype=f32),
            buf(seq, wide, dtype=f32),
            buf(seq, wide, dtype=f32),
            buf(seq, wide, dtype=f32),
            buf(*shapes[3]),
            buf(*shapes[3], dtype=f32),
        ]
        + [dma((4, height - 1))] * 4
        + [dma((4, height))] * 2
        + [dma((2, n_t - 1))] * 2
        + [dma((4, height))] * 2
        + [dma((4, height - 1))] * 2
        + [dma((3, n_t - 1))] * 2
        + [dma((n_vs,))] * 2,
        compiler_params=pltpu.CompilerParams(
            collective_id=2, has_side_effects=True, vmem_limit_bytes=63 * 1024 * 1024
        ),
        name="fused_layer",
    )(*weights, *rows, *vectors, *tables)


def hand_on(results, n_copied):
    hbm = pl.BlockSpec(memory_space=pl.ANY)
    vmem = pl.BlockSpec(memory_space=pltpu.VMEM)
    large, vec = results[:n_copied], results[n_copied]
    share = vec.shape[1]
    rows = (0, 1, 2, 3, 4, 4)

    def kernel(*refs):
        large_in, vec_in = refs[:n_copied], refs[n_copied]
        large_out = refs[n_copied + 1 : 2 * n_copied + 1]
        rows_out = refs[2 * n_copied + 1 : 2 * n_copied + 1 + len(rows)]
        held = refs[2 * n_copied + 1 + len(rows) : -2]
        in_sem, out_sem = refs[-2:]
        ins = [pltpu.make_async_copy(large_in[i], held[i], in_sem.at[i]) for i in range(n_copied)]
        outs = [pltpu.make_async_copy(held[i], large_out[i], out_sem.at[i]) for i in range(n_copied)]
        for copy in ins:
            copy.start()
        for i, row in enumerate(rows):
            rows_out[i][...] = vec_in[row : row + 1, :]
        for i in range(n_copied):
            ins[i].wait()
            outs[i].start()
        for copy in outs:
            copy.wait()

    return pl.pallas_call(
        kernel,
        out_shape=[jax.ShapeDtypeStruct(r.shape, r.dtype) for r in large]
        + [jax.ShapeDtypeStruct((1, share), vec.dtype) for _ in rows],
        in_specs=[hbm] * n_copied + [vmem],
        out_specs=[hbm] * n_copied + [vmem] * len(rows),
        scratch_shapes=[pltpu.VMEM(r.shape, r.dtype) for r in large]
        + [pltpu.SemaphoreType.DMA((n_copied,))] * 2,
        name="hand_on",
    )(*large, vec)


def contract_rows(left, right):
    return dot(left, right, ((0,), (0,)))


def contract_cols(left, right):
    return dot(left, right, ((1,), (1,)))


def rotary_tables(pos_ids):
    half_rot = ROT // 2
    inverse = 10000.0 ** (-(jnp.arange(half_rot, dtype=jnp.float32) * 2.0) / ROT)
    angles = pos_ids.astype(jnp.float32)[:, None] * inverse[None, :]
    cos_tab = jnp.concatenate([jnp.cos(angles), jnp.cos(angles)], axis=-1)
    sine_tab = jnp.concatenate([jnp.sin(angles), jnp.sin(angles)], axis=-1)
    return (cos_tab, sine_tab)


def rotate(blocked, cos_tab, sine_tab):
    head_part = blocked[..., :ROT]
    low_half = head_part[..., : ROT // 2]
    high_half = head_part[..., ROT // 2 :]
    turned = jnp.concatenate([-high_half, low_half], axis=-1)
    spun_part = head_part * cos_tab[:, None, :] + turned * sine_tab[:, None, :]
    return jnp.concatenate([spun_part, blocked[..., ROT:]], axis=-1)


def unrotate(grad_part, cos_tab, sine_tab):
    head_part = grad_part[..., :ROT]
    scaled = head_part * sine_tab[:, None, :]
    back_turn = jnp.concatenate([scaled[..., ROT // 2 :], -scaled[..., : ROT // 2]], axis=-1)
    return jnp.concatenate(
        [head_part * cos_tab[:, None, :] + back_turn, grad_part[..., ROT:]], axis=-1
    )


def gelu_pair(pre_act):
    cdf = 0.5 * (1.0 + lax.erf(pre_act / math.sqrt(2.0)))
    pdf = jnp.exp(-0.5 * pre_act * pre_act) / math.sqrt(2.0 * math.pi)
    return pre_act * cdf, cdf + pre_act * pdf


def normalise(rows):
    center = rows - jnp.mean(rows, axis=-1, keepdims=True)
    inv_std = lax.rsqrt(jnp.mean(center * center, axis=-1, keepdims=True) + norm_eps)
    return center * inv_std, inv_std


def heads_einsum(spec, left, right):
    return jnp.einsum(spec, left, right, preferred_element_type=jnp.float32)


def shards(
    tokens,
    segments,
    positions,
    ln1_gain,
    ln1_bias,
    ln2_gain,
    ln2_bias,
    qkv_weight,
    qkv_bias,
    dense_weight,
    dense_bias,
    fc1_weight,
    fc1_bias,
    fc2_weight,
    fc2_bias,
    cotangent,
    *,
    n_dp,
    n_t,
):
    bf16 = jnp.bfloat16
    width = tokens.shape[1]
    group = tokens.shape[0]
    share = width // n_dp
    heads_wide = qkv_weight.shape[2]
    if share % 16 == 0:
        fused = fused_layer(
            (fc1_weight[0], fc2_weight[0].T, qkv_weight[0], dense_weight[0]),
            (tokens, cotangent),
            (ln1_gain, ln1_bias, ln2_gain, ln2_bias, qkv_bias, fc1_bias, dense_bias, fc2_bias),
            (segments[None, :], positions[None, :]),
            n_dp,
            n_t,
        )
        y_out, x_grad, g_up, g_down_t, g_qkv, g_dense, sum_qkv, sum_up, *owned = hand_on(
            (*fused[:6], *fused[7:9], fused[6]), 8
        )
        return (
            y_out,
            x_grad,
            *owned[:4],
            g_qkv[None],
            sum_qkv,
            g_dense[None],
            owned[4],
            g_up[None],
            sum_up,
            g_down_t.T[None],
            owned[5],
        )
    gain_a, bias_a, gain_m, bias_m = ln1_gain[0], ln1_bias[0], ln2_gain[0], ln2_bias[0]
    gathered = gather_all(
        (qkv_weight[0], dense_weight[0].T, fc1_weight[0], fc2_weight[0].T),
        (tokens, cotangent),
        n_dp,
        n_t,
    )
    w_qkv, w_dense_t, w_up, w_down_t = [g.reshape(width, -1) for g in gathered[:4]]
    seq_rows, grad_full = [g.reshape(n_t * group, width) for g in gathered[4:]]
    seq_len = seq_rows.shape[0]

    cos_tab, sine_tab = rotary_tables(positions)
    normed, _ = normalise(seq_rows.astype(jnp.float32))
    in_attn = (normed * gain_a + bias_a).astype(bf16)
    in_mlp = (normed * gain_m + bias_m).astype(bf16)

    joined = (dot(in_attn, w_qkv, ((1,), (0,))) + qkv_bias[0]).reshape(seq_len, -1, 3, HEAD_DIM)
    queries = rotate(joined[:, :, 0], cos_tab, sine_tab).astype(bf16)
    key_rows = rotate(joined[:, :, 1], cos_tab, sine_tab).astype(bf16)
    value_rows = joined[:, :, 2].astype(bf16)

    score_scale = HEAD_DIM ** (-0.5)
    places_in = jnp.arange(seq_len, dtype=jnp.int32)
    allowed = (
        (segments[:, None] == segments[None, :]) & (places_in[:, None] >= places_in[None, :])
    )[None]
    scores = heads_einsum("qhd,khd->hqk", queries, key_rows) * score_scale
    scores = jnp.where(allowed, scores, -1e30)
    row_max = jnp.max(scores, axis=-1, keepdims=True)
    row_total = jnp.sum(jnp.exp(scores - row_max), axis=-1, keepdims=True)
    log_total = row_max + jnp.log(row_total)
    prob_wide = jnp.where(allowed, jnp.exp(scores - log_total), 0.0)
    probs = prob_wide.astype(bf16)
    context = heads_einsum("hqk,khd->qhd", probs, value_rows).reshape(seq_len, -1).astype(bf16)

    pre_act = dot(in_mlp, w_up, ((1,), (0,))) + fc1_bias[0]
    hidden, slope = gelu_pair(pre_act)
    hidden = hidden.astype(bf16)
    branch = contract_cols(context, w_dense_t) + contract_cols(hidden, w_down_t)

    grad_w_dense_t = contract_rows(grad_full, context)
    grad_w_down_t = contract_rows(grad_full, hidden)
    grad_pre = dot(grad_full, w_down_t, ((1,), (0,))) * slope
    grad_b_up = jnp.sum(grad_pre, axis=0)
    grad_pre_bf = grad_pre.astype(bf16)
    grad_ctx = dot(grad_full, w_dense_t, ((1,), (0,))).astype(bf16).reshape(seq_len, -1, HEAD_DIM)
    grad_w_up = contract_rows(in_mlp, grad_pre_bf)

    grad_probs = heads_einsum("qhd,khd->hqk", grad_ctx, value_rows)
    row_dot = jnp.sum(prob_wide * grad_probs, axis=-1, keepdims=True)
    grad_scores = (prob_wide * (grad_probs - row_dot) * score_scale).astype(bf16)
    grad_q = heads_einsum("hqk,khd->qhd", grad_scores, key_rows)
    grad_k = heads_einsum("hqk,qhd->khd", grad_scores, queries)
    grad_v = heads_einsum("hqk,qhd->khd", probs, grad_ctx)
    grad_joined = jnp.stack(
        [unrotate(grad_q, cos_tab, sine_tab), unrotate(grad_k, cos_tab, sine_tab), grad_v], axis=2
    ).reshape(seq_len, -1)
    grad_b_qkv = jnp.sum(grad_joined, axis=0)
    grad_joined_bf = grad_joined.astype(bf16)
    grad_w_qkv = contract_rows(in_attn, grad_joined_bf)

    part_attn = contract_cols(grad_joined_bf, w_qkv)
    part_mlp = contract_cols(grad_pre_bf, w_up)
    grad_rows = cotangent.astype(jnp.float32)
    heads_wide = grad_b_qkv.shape[0]
    n_vec = max(width, heads_wide, grad_b_up.shape[0])

    def lane(v):
        return jnp.pad(v, (0, n_vec - v.shape[0]))

    vec = jnp.stack(
        [
            lane(jnp.sum(part_attn * normed, axis=0)),
            lane(jnp.sum(part_attn, axis=0)),
            lane(jnp.sum(part_mlp * normed, axis=0)),
            lane(jnp.sum(part_mlp, axis=0)),
            lane(jnp.sum(grad_rows, axis=0)),
            lane(grad_b_qkv),
            lane(grad_b_up),
            jnp.zeros((n_vec,), jnp.float32),
        ]
    )

    def blocks(grad):
        return grad.astype(bf16).reshape(n_dp, width // n_dp, -1)

    def groups(part):
        return part.astype(bf16).reshape(n_t, group, width)

    (g_qkv, g_dense_t, g_up, g_down_t, mixed, grad_in_attn, grad_in_mlp, vec_sums) = reduce_all(
        (blocks(grad_w_qkv), blocks(grad_w_dense_t), blocks(grad_w_up), blocks(grad_w_down_t)),
        (groups(branch), groups(part_attn), groups(part_mlp)),
        vec,
        n_dp,
        n_t,
    )

    own_rows = tokens.astype(jnp.float32)
    own_normed, inv_std = normalise(own_rows)
    y_out = own_rows + mixed + dense_bias[0] + fc2_bias[0]
    grad_normed = grad_in_attn * gain_a + grad_in_mlp * gain_m
    x_grad = grad_rows + inv_std * (
        grad_normed
        - jnp.mean(grad_normed, axis=-1, keepdims=True)
        - own_normed * jnp.mean(grad_normed * own_normed, axis=-1, keepdims=True)
    )
    share = width // n_dp
    owned = lax.dynamic_slice_in_dim(vec_sums[1], lax.axis_index("dp") * share, share, axis=1)
    return (
        y_out,
        x_grad,
        owned[0:1],
        owned[1:2],
        owned[2:3],
        owned[3:4],
        g_qkv[None],
        vec_sums[0, 5:6, :heads_wide],
        g_dense_t.T[None],
        owned[4:5],
        g_up[None],
        vec_sums[0, 6:7, : grad_b_up.shape[0]],
        g_down_t.T[None],
        owned[4:5],
    )


def solution(mesh):
    placed = (
        P(("dp", "tensor"), None),
        P("dp"),
        P("dp"),
        P(),
        P(),
        P(),
        P(),
        P(None, "dp", "tensor"),
        P(None, "tensor"),
        P(None, "tensor", "dp"),
        P(),
        P(None, "dp", "tensor"),
        P(None, "tensor"),
        P(None, "tensor", "dp"),
        P(),
        P(("dp", "tensor"), None),
    )

    def step(*args):
        return shards(*args, n_dp=mesh.shape["dp"], n_t=mesh.shape["tensor"])

    return jax.shard_map(
        step,
        mesh=mesh,
        in_specs=placed,
        out_specs=(
            P(("dp", "tensor"), None),
            P(("dp", "tensor"), None),
            P(None, "dp"),
            P(None, "dp"),
            P(None, "dp"),
            P(None, "dp"),
            P(None, "dp", "tensor"),
            P(None, "tensor"),
            P(None, "tensor", "dp"),
            P(None, "dp"),
            P(None, "dp", "tensor"),
            P(None, "tensor"),
            P(None, "tensor", "dp"),
            P(None, "dp"),
        ),
        check_vma=False,
    )
```

```python
import math

import jax
import jax.numpy as jnp
from jax import lax
from jax.experimental import pallas as pl
from jax.experimental.pallas import tpu as pltpu
from jax.sharding import PartitionSpec as P

HEAD_DIM = 64
ROT = 16
PAIR = 2
MESH = pl.DeviceIdType.MESH
TURNS = (2, 1, 3)

norm_eps = 1e-05


def places(n_dp, n_t):
    dp = lax.axis_index("dp")
    t = lax.axis_index("tensor")
    return dp, t, dp // PAIR, lax.rem(dp, PAIR), n_dp // PAIR


def greet(devices):
    barrier = pltpu.get_barrier_semaphore()
    for device, there in devices:
        if there is None:
            pl.semaphore_signal(barrier, inc=1, device_id=device, device_id_type=MESH)
        else:

            @pl.when(there)
            def _(device=device):
                pl.semaphore_signal(barrier, inc=1, device_id=device, device_id_type=MESH)

    expected = sum(1 if there is None else there.astype(jnp.int32) for _, there in devices)
    pl.semaphore_wait(barrier, expected)


def gather_kernel(n_dp, n_t, n_w, *refs):
    w_in = refs[:n_w]
    rows_in = refs[n_w : n_w + 2]
    w_out = refs[n_w + 2 : 2 * n_w + 2]
    rows_out = refs[2 * n_w + 2 : 2 * n_w + 4]
    r_send, r_recv, l_send, l_recv, y_send, y_recv, t_send, t_recv = refs[2 * n_w + 4 :]
    dp, t, z, y, height = places(n_dp, n_t)
    mate = (z * PAIR + (1 - y), t)
    right = (jnp.minimum(z + 1, height - 1) * PAIR + y, t)
    left = (jnp.maximum(z - 1, 0) * PAIR + y, t)
    has_right = z + 1 < height
    has_left = z >= 1
    greet(
        [(mate, None), (right, has_right), (left, has_left)]
        + [((dp, lax.rem(t + k, n_t)), None) for k in range(1, n_t)]
    )

    def line(src, a, block, step, send, recv, device):
        return pltpu.make_async_remote_copy(
            src_ref=src,
            dst_ref=w_out[a].at[block * PAIR + y],
            send_sem=send.at[a, step],
            recv_sem=recv.at[a, step],
            device_id=device,
            device_id_type=MESH,
        )

    def across(src, a, block, side):
        return pltpu.make_async_remote_copy(
            src_ref=src,
            dst_ref=w_out[a].at[block * PAIR + side],
            send_sem=y_send.at[a, block],
            recv_sem=y_recv.at[a, block],
            device_id=mate,
            device_id_type=MESH,
        )

    def peer_copy(i, k, owner):
        return pltpu.make_async_remote_copy(
            src_ref=rows_in[i],
            dst_ref=rows_out[i].at[owner],
            send_sem=t_send.at[i, k - 1],
            recv_sem=t_recv.at[i, k - 1],
            device_id=(dp, lax.rem(t + k, n_t)),
            device_id_type=MESH,
        )

    for a in range(n_w):

        @pl.when(has_right)
        def _(a=a):
            line(w_in[a], a, z, 0, r_send, r_recv, right).start()

        @pl.when(has_left)
        def _(a=a):
            line(w_in[a], a, z, 0, l_send, l_recv, left).start()

        across(w_in[a], a, z, y).start()
    for i in range(2):
        for k in range(1, n_t):
            peer_copy(i, k, t).start()
    for a in range(n_w):
        w_out[a][dp] = w_in[a][...]
    for i in range(2):
        rows_out[i][t] = rows_in[i][...]

    for step in range(height - 1):
        for a in range(n_w):
            from_left = z - 1 - step
            from_right = z + 1 + step

            @pl.when(from_left >= 0)
            def _(a=a, block=from_left, step=step):
                held = w_out[a].at[block * PAIR + y]
                line(held, a, block, step, r_send, r_recv, right).wait_recv()
                across(held, a, block, y).start()
                if step + 1 < height - 1:

                    @pl.when(has_right)
                    def _():
                        line(held, a, block, step + 1, r_send, r_recv, right).start()

            @pl.when(from_right < height)
            def _(a=a, block=from_right, step=step):
                held = w_out[a].at[block * PAIR + y]
                line(held, a, block, step, l_send, l_recv, left).wait_recv()
                across(held, a, block, y).start()
                if step + 1 < height - 1:

                    @pl.when(has_left)
                    def _():
                        line(held, a, block, step + 1, l_send, l_recv, left).start()

    for i in range(2):
        for k in range(1, n_t):
            peer_copy(i, k, lax.rem(t + n_t - k, n_t)).wait_recv()
            peer_copy(i, k, t).wait_send()
    for a in range(n_w):
        for step in range(height - 1):

            @pl.when((z - step >= 0) & has_right)
            def _(a=a, step=step):
                line(w_in[a], a, z, step, r_send, r_recv, right).wait_send()

            @pl.when((z + step < height) & has_left)
            def _(a=a, step=step):
                line(w_in[a], a, z, step, l_send, l_recv, left).wait_send()

        for block in range(height):
            across(w_in[a], a, block, y).wait_send()
            across(w_in[a], a, block, 1 - y).wait_recv()


def gather_all(weights, rows, n_dp, n_t):
    n_w = len(weights)
    height = n_dp // PAIR
    vmem = pl.BlockSpec(memory_space=pltpu.VMEM)
    dma = pltpu.SemaphoreType.DMA

    def kernel(*refs):
        gather_kernel(n_dp, n_t, n_w, *refs)

    return pl.pallas_call(
        kernel,
        out_shape=[jax.ShapeDtypeStruct((n_dp,) + w.shape, w.dtype) for w in weights]
        + [jax.ShapeDtypeStruct((n_t,) + r.shape, r.dtype) for r in rows],
        in_specs=[vmem] * (n_w + 2),
        out_specs=[vmem] * (n_w + 2),
        scratch_shapes=[
            dma((n_w, height - 1)),
            dma((n_w, height - 1)),
            dma((n_w, height - 1)),
            dma((n_w, height - 1)),
            dma((n_w, height)),
            dma((n_w, height)),
            dma((2, n_t - 1)),
            dma((2, n_t - 1)),
        ],
        compiler_params=pltpu.CompilerParams(collective_id=0, has_side_effects=True),
        name="gather_all",
    )(*weights, *rows)


def reduce_kernel(n_dp, n_t, n_w, n_r, *refs):
    g_in = refs[:n_w]
    p_in = refs[n_w : n_w + n_r]
    vec_in = refs[n_w + n_r]
    base = n_w + n_r + 1
    g_out = refs[base : base + n_w]
    p_out = refs[base + n_w : base + n_w + n_r]
    vec_out = refs[base + n_w + n_r]
    base = 2 * base
    y_buf = refs[base : base + n_w]
    s_buf = refs[base + n_w : base + 2 * n_w]
    z_buf = refs[base + 2 * n_w : base + 3 * n_w]
    base += 3 * n_w
    p_buf = refs[base : base + n_r]
    vy_buf, vs_buf, vz_buf, vd_buf, vt_buf = refs[base + n_r : base + n_r + 5]
    (
        y_send,
        y_recv,
        z_send,
        z_recv,
        p_send,
        p_recv,
        v_send,
        v_recv,
    ) = refs[base + n_r + 5 :]
    dp, t, z, y, height = places(n_dp, n_t)
    mate = (z * PAIR + (1 - y), t)

    def at_z(k):
        return lax.rem(z + k, height)

    greet(
        [(mate, None)]
        + [((at_z(k) * PAIR + y, t), None) for k in range(1, height)]
        + [((dp, lax.rem(t + k, n_t)), None) for k in range(1, n_t)]
    )

    def remote(src, dst, send, recv, device):
        return pltpu.make_async_remote_copy(
            src_ref=src,
            dst_ref=dst,
            send_sem=send,
            recv_sem=recv,
            device_id=device,
            device_id_type=MESH,
        )

    order = [k for k in range(1, height)] + [0]

    def swap(a, k):
        return remote(
            g_in[a].at[at_z(k) * PAIR + (1 - y)],
            y_buf[a].at[k],
            y_send.at[a, k],
            y_recv.at[a, k],
            mate,
        )

    def to_owner(a, k):
        return remote(
            s_buf[a].at[k - 1],
            z_buf[a].at[k - 1],
            z_send.at[a, k - 1],
            z_recv.at[a, k - 1],
            (at_z(k) * PAIR + y, t),
        )

    def to_peer(i, k):
        return remote(
            p_in[i].at[lax.rem(t + k, n_t)],
            p_buf[i].at[k - 1],
            p_send.at[i, k - 1],
            p_recv.at[i, k - 1],
            (dp, lax.rem(t + k, n_t)),
        )

    vec_swap = remote(vec_in, vy_buf, v_send.at[0], v_recv.at[0], mate)

    def vec_owner(k):
        return remote(
            vs_buf, vz_buf.at[k - 1], v_send.at[k], v_recv.at[k], (at_z(k) * PAIR + y, t)
        )

    def vec_peer(k):
        at = height - 1 + k
        return remote(
            vd_buf, vt_buf.at[k - 1], v_send.at[at], v_recv.at[at], (dp, lax.rem(t + k, n_t))
        )

    vec_swap.start()
    for k in order:
        for a in range(n_w):
            swap(a, k).start()
    for i in range(n_r):
        for k in range(1, n_t):
            to_peer(i, k).start()

    vec_swap.wait_recv()
    vs_buf[...] = vec_in[...] + vy_buf[...]
    for k in range(1, height):
        vec_owner(k).start()

    for k in range(1, height):
        for a in range(n_w):
            swap(a, k).wait_recv()
            own = g_in[a][at_z(k) * PAIR + y].astype(jnp.float32)
            s_buf[a][k - 1] = (own + y_buf[a][k].astype(jnp.float32)).astype(jnp.bfloat16)
            to_owner(a, k).start()
        if k == 1:
            total = vs_buf[...]
            for j in range(1, height):
                vec_owner(j).wait_recv()
                total = total + vz_buf[j - 1]
            vd_buf[...] = total
            for j in range(1, n_t):
                vec_peer(j).start()

    for i in range(n_r):
        total = p_in[i][t].astype(jnp.float32)
        for k in range(1, n_t):
            to_peer(i, k).wait_recv()
            total = total + p_buf[i][k - 1].astype(jnp.float32)
        p_out[i][...] = total

    total = vd_buf[...]
    for k in range(1, n_t):
        vec_peer(k).wait_recv()
        total = total + vt_buf[k - 1]
    vec_out[0] = vd_buf[...]
    vec_out[1] = total

    for a in range(n_w):
        swap(a, 0).wait_recv()
        total = g_in[a][dp].astype(jnp.float32) + y_buf[a][0].astype(jnp.float32)
        g_out[a][...] = total
    for k in range(1, height):
        for a in range(n_w):
            to_owner(a, k).wait_recv()
            g_out[a][...] += z_buf[a][k - 1].astype(jnp.float32)

    vec_swap.wait_send()
    for k in range(1, height):
        vec_owner(k).wait_send()
    for k in range(1, n_t):
        vec_peer(k).wait_send()
    for a in range(n_w):
        for k in range(height):
            swap(a, k).wait_send()
        for k in range(1, height):
            to_owner(a, k).wait_send()
    for i in range(n_r):
        for k in range(1, n_t):
            to_peer(i, k).wait_send()


def reduce_all(grads, parts, vec, n_dp, n_t):
    n_w, n_r = len(grads), len(parts)
    height = n_dp // PAIR
    vmem = pl.BlockSpec(memory_space=pltpu.VMEM)
    dma = pltpu.SemaphoreType.DMA

    def kernel(*refs):
        reduce_kernel(n_dp, n_t, n_w, n_r, *refs)

    n_in = n_w + n_r + 1
    n_vec = height + n_t - 1
    return pl.pallas_call(
        kernel,
        out_shape=[jax.ShapeDtypeStruct(g.shape[1:], jnp.float32) for g in grads]
        + [jax.ShapeDtypeStruct(p.shape[1:], jnp.float32) for p in parts]
        + [jax.ShapeDtypeStruct((2,) + vec.shape, jnp.float32)],
        in_specs=[vmem] * n_in,
        out_specs=[vmem] * n_in,
        scratch_shapes=[pltpu.VMEM((height,) + g.shape[1:], jnp.bfloat16) for g in grads]
        + [pltpu.VMEM((height - 1,) + g.shape[1:], jnp.bfloat16) for g in grads]
        + [pltpu.VMEM((height - 1,) + g.shape[1:], jnp.bfloat16) for g in grads]
        + [pltpu.VMEM((n_t - 1,) + p.shape[1:], jnp.bfloat16) for p in parts]
        + [
            pltpu.VMEM(vec.shape, jnp.float32),
            pltpu.VMEM(vec.shape, jnp.float32),
            pltpu.VMEM((height - 1,) + vec.shape, jnp.float32),
            pltpu.VMEM(vec.shape, jnp.float32),
            pltpu.VMEM((n_t - 1,) + vec.shape, jnp.float32),
        ]
        + [
            dma((n_w, height)),
            dma((n_w, height)),
            dma((n_w, height - 1)),
            dma((n_w, height - 1)),
            dma((n_r, n_t - 1)),
            dma((n_r, n_t - 1)),
            dma((n_vec,)),
            dma((n_vec,)),
        ],
        compiler_params=pltpu.CompilerParams(collective_id=1, has_side_effects=True),
        name="reduce_all",
    )(*grads, *parts, vec)


def dot(left, right, dims):
    return lax.dot_general(left, right, (dims, ((), ())), preferred_element_type=jnp.float32)


NN = ((1,), (0,))
NT = ((1,), (1,))
TN = ((0,), (0,))


def fused_kernel(n_dp, n_t, cuts, extra, refs):
    bf16, f32 = jnp.bfloat16, jnp.float32
    (
        w_up_in,
        w_down_in,
        w_qkv_in,
        w_dense_in,
        tok_in,
        cot_in,
        gain_a,
        bias_a,
        gain_m,
        bias_m,
        b_qkv,
        b_up,
        b_dense,
        b_down,
        seg_row,
        pos_row,
        y_ref,
        x_ref,
        g_up,
        g_down,
        g_qkv,
        g_dense,
        vec_out,
        qkv_bias_out,
        up_bias_out,
    ) = refs[:25]
    rest = list(refs[25:])

    def take(n):
        got = rest[:n]
        del rest[:n]
        return got

    n_p = 1 + 2 * (len(cuts) - 1)
    w_all, g_in, y_buf, s_buf, z_buf = take(n_p), take(n_p), take(n_p), take(n_p), take(n_p)
    rows_all, p_in, pc_buf, px_out, px_buf = take(2), take(3), take(3), take(3), take(3)
    vec_in, vy_buf, vs_buf, vz_buf, vd_buf, vt_buf = take(6)
    normed, in_a, in_m, in_at, in_mt, grad_t, hidden, grad_pre, joined, cos_w, sin_a, sin_b = take(12)
    w_att, g_att = take(2)
    r_send, r_recv, l_send, l_recv, rb_send, rb_recv, lb_send, lb_recv, f_send, f_recv = take(10)
    y_send, y_recv, z_send, z_recv = take(4)
    t_send, t_recv, p_send, p_recv, v_send, v_recv = take(6)

    dp, t, z, y, height = places(n_dp, n_t)
    group, width = tok_in.shape
    share = w_up_in.shape[0]
    near = share - extra
    seq = group * n_t
    wide = joined.shape[1]
    heads_wide = w_qkv_in.shape[1]
    n_heads = heads_wide // (3 * HEAD_DIM)
    mate = (z * PAIR + (1 - y), t)
    right = (jnp.minimum(z + 1, height - 1) * PAIR + y, t)
    left = (jnp.maximum(z - 1, 0) * PAIR + y, t)
    has_right = z + 1 < height
    has_left = z >= 1
    side, core = t // 2, lax.rem(t, 2)
    twin = (dp, side * 2 + (1 - core))
    over = (dp, (1 - side) * 2 + core)

    def at_z(k):
        return lax.rem(z + k, height)

    def z_device(k):
        return (at_z(k) * PAIR + y, t)

    def t_device(k):
        return (dp, lax.rem(t + k, n_t))

    greet(
        [(mate, None)]
        + [(z_device(k), None) for k in range(1, height)]
        + [(t_device(k), None) for k in range(1, n_t)]
    )

    def remote(src, dst, send, recv, device):
        return pltpu.make_async_remote_copy(
            src_ref=src,
            dst_ref=dst,
            send_sem=send,
            recv_sem=recv,
            device_id=device,
            device_id_type=MESH,
        )

    n_c = len(cuts) - 1
    w_in = [w_att]
    g_out = [g_att]
    for c in range(n_c):
        at = pl.ds(cuts[c], cuts[c + 1] - cuts[c])
        w_in += [w_up_in.at[:, at], w_down_in.at[:, at]]
        g_out += [g_up.at[:, at], g_down.at[:, at]]
    attn = (0,)
    chunk = [(1 + 2 * c, 2 + 2 * c) for c in range(n_c)]
    low_part = heads_wide // 128 * 128
    shift = heads_wide - low_part
    all_wide = w_att.shape[1]
    everything = tuple(range(n_p))

    tail_rows = pl.ds(near, extra)
    near_rows = pl.ds(0, near)

    def line(src, a, block, step, send, recv, device):
        return remote(
            src, w_all[a].at[block * PAIR + y], send.at[a, step], recv.at[a, step], device
        )

    def line_b(a, block, step, send, recv, device):
        held = w_all[a].at[block * PAIR + (1 - y), tail_rows]
        return remote(held, held, send.at[a, step], recv.at[a, step], device)

    def across_own(a, at):
        return remote(
            w_in[a], w_all[a].at[z * PAIR + at], f_send.at[a, z], f_recv.at[a, z], mate
        )

    def across(a, block, at):
        held = w_all[a].at[block * PAIR + at, near_rows]
        return remote(held, held, f_send.at[a, block], f_recv.at[a, block], mate)

    def send_own(arrays):
        for a in arrays:

            @pl.when(has_right)
            def _(a=a):
                line(w_in[a], a, z, 0, r_send, r_recv, right).start()

            @pl.when(has_left)
            def _(a=a):
                line(w_in[a], a, z, 0, l_send, l_recv, left).start()

            across_own(a, y).start()

    def send_mates(arrays):
        for a in arrays:
            across_own(a, 1 - y).wait_recv()

            @pl.when(has_right)
            def _(a=a):
                line_b(a, z, 0, rb_send, rb_recv, right).start()

            @pl.when(has_left)
            def _(a=a):
                line_b(a, z, 0, lb_send, lb_recv, left).start()

    def relay(step, arrays):
        for a in arrays:
            from_left = z - 1 - step
            from_right = z + 1 + step

            @pl.when(from_left >= 0)
            def _(a=a, block=from_left):
                held = w_all[a].at[block * PAIR + y]
                line(held, a, block, step, r_send, r_recv, right).wait_recv()
                if step + 1 < height - 1:

                    @pl.when(has_right)
                    def _():
                        line(held, a, block, step + 1, r_send, r_recv, right).start()

                across(a, block, y).start()

            @pl.when(from_right < height)
            def _(a=a, block=from_right):
                held = w_all[a].at[block * PAIR + y]
                line(held, a, block, step, l_send, l_recv, left).wait_recv()
                if step + 1 < height - 1:

                    @pl.when(has_left)
                    def _():
                        line(held, a, block, step + 1, l_send, l_recv, left).start()

                across(a, block, y).start()

        for a in arrays:

            @pl.when(z - 1 - step >= 0)
            def _(a=a, block=z - 1 - step):
                line_b(a, block, step, rb_send, rb_recv, right).wait_recv()
                if step + 1 < height - 1:

                    @pl.when(has_right)
                    def _():
                        line_b(a, block, step + 1, rb_send, rb_recv, right).start()

            @pl.when(z + 1 + step < height)
            def _(a=a, block=z + 1 + step):
                line_b(a, block, step, lb_send, lb_recv, left).wait_recv()
                if step + 1 < height - 1:

                    @pl.when(has_left)
                    def _():
                        line_b(a, block, step + 1, lb_send, lb_recv, left).start()

    def land(arrays):
        for a in arrays:
            for block in range(height):

                @pl.when(z != block)
                def _(a=a, block=block):
                    across(a, block, 1 - y).wait_recv()

    rows_in = (tok_in, cot_in)

    def row_copy(src, i, k, owner, device):
        return remote(src, rows_all[i].at[owner], t_send.at[i, k], t_recv.at[i, k], device)

    def swap(a, k):
        return remote(
            g_in[a].at[at_z(k) * PAIR + (1 - y)],
            y_buf[a].at[k],
            y_send.at[a, k],
            y_recv.at[a, k],
            mate,
        )

    def to_owner(a, k):
        return remote(
            s_buf[a].at[k - 1],
            z_buf[a].at[k - 1],
            z_send.at[a, k - 1],
            z_recv.at[a, k - 1],
            z_device(k),
        )

    turns = [k for k in TURNS if k < height] + [0]

    def swap_all(arrays):
        for k in turns:
            for a in arrays:
                swap(a, k).start()

    def wide_of(ref, *at):
        return ref[at].astype(f32)

    def settle(arrays, k):
        for a in arrays:
            swap(a, k).wait_recv()
            own = wide_of(g_in[a], at_z(k) * PAIR + y)
            s_buf[a][k - 1] = (own + wide_of(y_buf[a], k)).astype(bf16)
            to_owner(a, k).start()

    def close(arrays):
        for a in arrays:
            swap(a, 0).wait_recv()
            total = wide_of(g_in[a], dp) + wide_of(y_buf[a], 0)
            for k in turns[:-1]:
                to_owner(a, k).wait_recv()
                total = total + wide_of(z_buf[a], k - 1)
            g_out[a][...] = total

    def to_twin(i):
        return remote(p_in[i].at[1 - core], pc_buf[i], p_send.at[i, 0], p_recv.at[i, 0], twin)

    def to_over(i):
        return remote(px_out[i], px_buf[i], p_send.at[i, 1], p_recv.at[i, 1], over)

    def part_over(i):
        to_twin(i).wait_recv()
        px_out[i][...] = (
            wide_of(p_in[i], core, 1 - side) + wide_of(pc_buf[i], 1 - side)
        ).astype(bf16)
        to_over(i).start()

    def part_sum(i):
        to_over(i).wait_recv()
        return wide_of(p_in[i], core, side) + wide_of(pc_buf[i], side) + px_buf[i][...].astype(f32)

    vec_swap = remote(vec_in, vy_buf, v_send.at[0], v_recv.at[0], mate)

    def vec_owner(k):
        return remote(vs_buf, vz_buf.at[k - 1], v_send.at[k], v_recv.at[k], z_device(k))

    def vec_peer(k):
        at = height - 1 + k
        return remote(vd_buf, vt_buf.at[k - 1], v_send.at[at], v_recv.at[at], t_device(k))

    w_att[:, low_part:] = jnp.concatenate(
        [jnp.zeros((shift, share), bf16), w_dense_in[...]], axis=0
    ).T
    w_att[:, :heads_wide] = w_qkv_in[...]
    send_own(attn)
    for i in range(2):
        row_copy(rows_in[i], i, 0, t, over).start()
        row_copy(rows_in[i], i, 1, t, twin).start()
    for i in range(2):
        rows_all[i][t] = rows_in[i][...]
    for a in everything:
        w_all[a][dp] = w_in[a][...]

    send_own(chunk[0])
    send_mates(attn)
    relay(0, attn)

    lanes = lax.broadcasted_iota(jnp.int32, (8, wide), 1)
    subs = lax.broadcasted_iota(jnp.int32, (8, wide), 0)
    part = lax.rem(lanes, HEAD_DIM)
    kind = lax.rem(lanes // HEAD_DIM, 3)
    turning = (kind < 2) & (lanes < heads_wide)
    low = (turning & (part == subs)).astype(f32)
    high = (turning & (part == subs + ROT // 2)).astype(f32)
    still = 1.0 - jnp.sum(low + high, axis=0, keepdims=True)

    def spread(table, where):
        return lax.dot_general(
            table, where, (TN, ((), ())), preferred_element_type=f32, precision=lax.Precision.HIGHEST
        )

    half_rot = ROT // 2
    order = lax.broadcasted_iota(jnp.int32, (half_rot, seq), 0)
    inverse = jnp.zeros((half_rot, seq), f32)
    for i in range(half_rot):
        inverse = jnp.where(order == i, 10000.0 ** (-2.0 * i / ROT), inverse)
    angles = pos_row[...].astype(f32) * inverse
    cos8, sin8 = jnp.cos(angles), jnp.sin(angles)
    cos_w[...] = spread(cos8, low + high) + still
    sin_a[...] = -spread(sin8, low)
    sin_b[...] = spread(sin8, high)

    far = (1 - side) * 2
    for i in range(2):
        row_copy(rows_in[i], i, 0, far + core, over).wait_recv()
        row_copy(rows_all[i].at[far + core], i, 2, far + core, twin).start()
        if i == 0:
            relay(1, attn)
            send_mates(chunk[0])
    for i in range(2):
        row_copy(rows_in[i], i, 1, side * 2 + (1 - core), twin).wait_recv()
        row_copy(rows_in[i], i, 2, far + (1 - core), twin).wait_recv()

    def norm_of(rows):
        center = rows - jnp.mean(rows, axis=-1, keepdims=True)
        inv_std = lax.rsqrt(jnp.mean(center * center, axis=-1, keepdims=True) + norm_eps)
        return center * inv_std, inv_std

    for g in range(n_t):
        at = pl.ds(g * group, group)
        value, _ = norm_of(rows_all[0][g].astype(f32))
        normed[at, :] = value
        va = (value * gain_a[...] + bias_a[...]).astype(bf16)
        vm = (value * gain_m[...] + bias_m[...]).astype(bf16)
        in_a[at, :] = va
        in_m[at, :] = vm
        in_at[:, at] = va.T
        in_mt[:, at] = vm.T
        grad_t[:, at] = rows_all[1][g].T
        if g == 0:
            relay(2, attn)
            send_own(chunk[1])
    grad_full = rows_all[1][...].reshape(seq, width)
    land(attn)

    def blocks(grad):
        return grad.astype(bf16).reshape(n_dp, share, -1)

    def whole(a):
        return w_all[a][...].reshape(width, -1)

    vec_in[...] = jnp.zeros_like(vec_in)
    w_qkv = w_all[0][:, :, :wide].reshape(width, -1)
    w_dense = w_all[0][:, :, low_part:].reshape(width, -1)
    joined[...] = dot(in_a[...], w_qkv, NN)
    joined[:, :heads_wide] += b_qkv[...]
    joined[:, heads_wide:] = jnp.zeros((seq, wide - heads_wide), f32)

    def turn(value, sign):
        moved = pltpu.roll(value, wide - ROT // 2, 1) * sin_a[...]
        moved = moved + pltpu.roll(value, ROT // 2, 1) * sin_b[...]
        return value * cos_w[...] + sign * moved

    relay(0, chunk[0])
    turned = turn(joined[...], 1.0).astype(bf16)
    grad_ctx = dot(grad_full, w_dense, NN).astype(bf16)
    row_at = lax.broadcasted_iota(jnp.int32, (seq, seq), 0)
    col_at = lax.broadcasted_iota(jnp.int32, (seq, seq), 1)
    seg_at = seg_row[...].astype(f32)
    seg_col = jnp.broadcast_to(seg_at, (128, seq)).T[:, :1]
    allowed = (seg_col == seg_at) & (row_at >= col_at)
    scale = HEAD_DIM ** (-0.5)
    contexts = [jnp.zeros((seq, shift), bf16)]
    for h in range(n_heads):
        base = h * 3 * HEAD_DIM
        q = turned[:, base : base + HEAD_DIM]
        k_h = turned[:, base + HEAD_DIM : base + 2 * HEAD_DIM]
        v = turned[:, base + 2 * HEAD_DIM : base + 3 * HEAD_DIM]
        gc = grad_ctx[:, shift + h * HEAD_DIM : shift + (h + 1) * HEAD_DIM]
        scores = jnp.where(allowed, dot(q, k_h, NT) * scale, -1e30)
        e = jnp.exp(scores - jnp.max(scores, axis=-1, keepdims=True))
        p = e * (1.0 / jnp.sum(e, axis=-1, keepdims=True))
        pb = p.astype(bf16)
        contexts.append(dot(pb, v, NN).astype(bf16))
        gp = dot(gc, v, NT)
        row_dot = jnp.sum(p * gp, axis=-1, keepdims=True)
        gs = (p * (gp - row_dot) * scale).astype(bf16)
        joined[:, base : base + HEAD_DIM] = dot(gs, k_h, NN)
        joined[:, base + HEAD_DIM : base + 2 * HEAD_DIM] = dot(gs, q, TN)
        joined[:, base + 2 * HEAD_DIM : base + 3 * HEAD_DIM] = dot(pb, gc, TN)
        if h == 0:
            send_mates(chunk[1])
        if h == 1:
            relay(1, chunk[0])
    context = jnp.concatenate(contexts, axis=1)
    grad_joined = turn(joined[...], -1.0)
    vec_in[5:6, :wide] = jnp.sum(grad_joined, axis=0, keepdims=True)
    gj = grad_joined.astype(bf16)
    for_qkv = dot(in_at[...], gj, NN)
    for_dense = dot(grad_t[...], context, NN)
    g_in[0][:, :, :low_part] = blocks(for_qkv[:, :low_part])
    g_in[0][:, :, low_part:wide] = blocks(for_qkv[:, low_part:] + for_dense[:, : wide - low_part])
    g_in[0][:, :, wide:] = blocks(for_dense[:, wide - low_part :])
    swap_all(attn)
    relay(2, chunk[0])
    relay(0, chunk[1])

    def feed(c, g):
        at = pl.ds(g * group, group)
        cols = pl.ds(cuts[c], cuts[c + 1] - cuts[c])
        up, down = chunk[c]
        pre = dot(in_m[at, :], whole(up), NN) + b_up[:, cols]
        cdf = 0.5 * (1.0 + lax.erf(pre / math.sqrt(2.0)))
        pdf = jnp.exp(-0.5 * pre * pre) / math.sqrt(2.0 * math.pi)
        hidden[at, cols] = (pre * cdf).astype(bf16)
        gp = dot(rows_all[1][g], whole(down), NN) * (cdf + pre * pdf)
        vec_in[6:7, cols] += jnp.sum(gp, axis=0, keepdims=True)
        grad_pre[at, cols] = gp.astype(bf16)

    def feed_grads(c):
        cols = pl.ds(cuts[c], cuts[c + 1] - cuts[c])
        up, down = chunk[c]
        g_in[up][...] = blocks(dot(in_mt[...], grad_pre[:, cols], NN))
        swap_all((up,))
        g_in[down][...] = blocks(dot(grad_t[...], hidden[:, cols], NN))
        swap_all((down,))

    def units(c):
        return pl.ds(cuts[c], cuts[c + 1] - cuts[c])

    land(chunk[0])
    for g in range(n_t):
        feed(0, g)
        if g == 1:
            relay(1, chunk[1])
    relay(2, chunk[1])
    feed_grads(0)
    settle(attn, turns[0])
    for g in range(n_t):
        at = pl.ds(g * group, group)
        pa = dot(gj[g * group : (g + 1) * group], w_qkv, NT)
        vec_in[0:1, :width] += jnp.sum(pa * normed[at, :], axis=0, keepdims=True)
        vec_in[1:2, :width] += jnp.sum(pa, axis=0, keepdims=True)
        p_in[1][g % 2, g // 2] = pa.astype(bf16)
    to_twin(1).start()
    settle(attn, turns[1])
    grad_rows = cot_in[...].astype(f32)
    vec_in[4:5, :width] = jnp.sum(grad_rows, axis=0, keepdims=True)
    land(chunk[1])
    for g in range(n_t):
        feed(1, g)
        if g == 1:
            settle(attn, turns[2])
    part_over(1)
    for g in range(n_t):
        at = pl.ds(g * group, group)
        pm = dot(grad_pre[at, units(0)], whole(chunk[0][0]), NT)
        for c in range(1, n_c):
            pm = pm + dot(grad_pre[at, units(c)], whole(chunk[c][0]), NT)
        vec_in[2:3, :width] += jnp.sum(pm * normed[at, :], axis=0, keepdims=True)
        vec_in[3:4, :width] += jnp.sum(pm, axis=0, keepdims=True)
        p_in[2][g % 2, g // 2] = pm.astype(bf16)
    vec_swap.start()
    to_twin(2).start()
    feed_grads(1)
    settle(chunk[0], turns[0])
    for g in range(n_t):
        at = pl.ds(g * group, group)
        branch = dot(context[g * group : (g + 1) * group], w_dense, NT)
        for c in range(n_c):
            branch = branch + dot(hidden[at, units(c)], whole(chunk[c][1]), NT)
        p_in[0][g % 2, g // 2] = branch.astype(bf16)
    to_twin(0).start()
    part_over(2)
    settle(chunk[0], turns[1])
    part_over(0)
    close(attn)
    g_qkv[...] = g_att[:, :heads_wide]
    g_dense[...] = g_att[:, low_part:].T[shift:]
    settle(chunk[0], turns[2])
    vec_swap.wait_recv()
    vs_buf[...] = vec_in[...] + vy_buf[...]
    for j in range(1, height):
        vec_owner(j).start()
    settle(chunk[1], turns[0])
    settle(chunk[1], turns[1])
    total = vs_buf[...]
    for j in range(1, height):
        vec_owner(j).wait_recv()
        total = total + vz_buf[j - 1]
    vd_buf[...] = total
    for j in range(1, n_t):
        vec_peer(j).start()
    settle(chunk[1], turns[2])
    own = tok_in[...].astype(f32)
    own_normed, inv_std = norm_of(own)
    grad_normed = part_sum(1) * gain_a[...] + part_sum(2) * gain_m[...]
    x_ref[...] = grad_rows + inv_std * (
        grad_normed
        - jnp.mean(grad_normed, axis=-1, keepdims=True)
        - own_normed * jnp.mean(grad_normed * own_normed, axis=-1, keepdims=True)
    )
    y_ref[...] = own + part_sum(0) + b_dense[...] + b_down[...]
    total = vd_buf[...]
    for k in range(1, n_t):
        vec_peer(k).wait_recv()
        total = total + vt_buf[k - 1]
    owned = jnp.zeros((8, share), f32)
    for d in range(n_dp):
        owned = jnp.where(dp == d, total[:, d * share : (d + 1) * share], owned)
    vec_out[...] = owned
    qkv_bias_out[...] = vd_buf[5:6, :heads_wide]
    up_bias_out[...] = vd_buf[6:7, : w_up_in.shape[1]]
    close(chunk[0])
    close(chunk[1])

    for i in range(2):
        row_copy(rows_in[i], i, 0, t, over).wait_send()
        row_copy(rows_in[i], i, 1, t, twin).wait_send()
        row_copy(rows_in[i], i, 2, t, twin).wait_send()
    for a in everything:
        for step in range(height - 1):

            @pl.when((z - step >= 0) & has_right)
            def _(a=a, step=step):
                line(w_in[a], a, z, step, r_send, r_recv, right).wait_send()
                line_b(a, z, step, rb_send, rb_recv, right).wait_send()

            @pl.when((z + step < height) & has_left)
            def _(a=a, step=step):
                line(w_in[a], a, z, step, l_send, l_recv, left).wait_send()
                line_b(a, z, step, lb_send, lb_recv, left).wait_send()

        across_own(a, y).wait_send()
        for block in range(height):

            @pl.when(z != block)
            def _(a=a, block=block):
                across(a, block, y).wait_send()

        for k in range(height):
            swap(a, k).wait_send()
        for k in range(1, height):
            to_owner(a, k).wait_send()
    vec_swap.wait_send()
    for k in range(1, height):
        vec_owner(k).wait_send()
    for k in range(1, n_t):
        vec_peer(k).wait_send()
    for i in range(3):
        to_twin(i).wait_send()
        to_over(i).wait_send()


def fused_layer(weights, rows, vectors, tables, n_dp, n_t):
    height = n_dp // PAIR
    bf16, f32 = jnp.bfloat16, jnp.float32
    group, width = rows[0].shape
    seq = group * n_t
    share = weights[0].shape[0]
    extra = share // 48 * 16
    heads_wide = weights[2].shape[1]
    wide = -(-heads_wide // 128) * 128
    units = weights[0].shape[1]
    cuts = (0, units // 3 * 2, units)
    n_vec = max(width, heads_wide, units)
    vmem = pl.BlockSpec(memory_space=pltpu.VMEM)
    dma = pltpu.SemaphoreType.DMA
    n_vs = height + n_t - 1
    widths = [heads_wide + weights[3].shape[0]]
    for c in range(len(cuts) - 1):
        widths += [cuts[c + 1] - cuts[c]] * 2
    n_p = len(widths)

    def buf(*shape, dtype=bf16):
        return pltpu.VMEM(shape, dtype)

    def per_piece(*lead):
        return [buf(*lead, w) for w in widths]

    def kernel(*refs):
        fused_kernel(n_dp, n_t, cuts, extra, refs)

    return pl.pallas_call(
        kernel,
        out_shape=[jax.ShapeDtypeStruct((group, width), f32)] * 2
        + [jax.ShapeDtypeStruct(w.shape, f32) for w in weights]
        + [
            jax.ShapeDtypeStruct((8, share), f32),
            jax.ShapeDtypeStruct((1, heads_wide), f32),
            jax.ShapeDtypeStruct((1, units), f32),
        ],
        in_specs=[vmem] * 16,
        out_specs=[vmem] * 9,
        scratch_shapes=per_piece(n_dp, share)
        + per_piece(n_dp, share)
        + per_piece(height, share)
        + per_piece(height - 1, share)
        + per_piece(height - 1, share)
        + [buf(n_t, group, width)] * 2
        + [buf(2, 2, group, width)] * 3
        + [buf(2, group, width)] * 3
        + [buf(group, width)] * 6
        + [
            buf(8, n_vec, dtype=f32),
            buf(8, n_vec, dtype=f32),
            buf(8, n_vec, dtype=f32),
            buf(height - 1, 8, n_vec, dtype=f32),
            buf(8, n_vec, dtype=f32),
            buf(n_t - 1, 8, n_vec, dtype=f32),
            buf(seq, width, dtype=f32),
            buf(seq, width),
            buf(seq, width),
            buf(width, seq),
            buf(width, seq),
            buf(width, seq),
            buf(seq, units),
            buf(seq, units),
            buf(seq, wide, dtype=f32),
            buf(seq, wide, dtype=f32),
            buf(seq, wide, dtype=f32),
            buf(seq, wide, dtype=f32),
            buf(share, widths[0]),
            buf(share, widths[0], dtype=f32),
        ]
        + [dma((n_p, height - 1))] * 8
        + [dma((n_p, height))] * 2
        + [dma((n_p, height))] * 2
        + [dma((n_p, height - 1))] * 2
        + [dma((2, 3))] * 2
        + [dma((3, 2))] * 2
        + [dma((n_vs,))] * 2,
        compiler_params=pltpu.CompilerParams(
            collective_id=2, has_side_effects=True, vmem_limit_bytes=63 * 1024 * 1024
        ),
        name="fused_layer",
    )(*weights, *rows, *vectors, *tables)


def hand_on(results, n_copied):
    hbm = pl.BlockSpec(memory_space=pl.ANY)
    vmem = pl.BlockSpec(memory_space=pltpu.VMEM)
    large, vec = results[:n_copied], results[n_copied]
    share = vec.shape[1]
    rows = (0, 1, 2, 3, 4, 4)

    def kernel(*refs):
        large_in, vec_in = refs[:n_copied], refs[n_copied]
        large_out = refs[n_copied + 1 : 2 * n_copied + 1]
        rows_out = refs[2 * n_copied + 1 : 2 * n_copied + 1 + len(rows)]
        held = refs[2 * n_copied + 1 + len(rows) : -2]
        in_sem, out_sem = refs[-2:]
        ins = [pltpu.make_async_copy(large_in[i], held[i], in_sem.at[i]) for i in range(n_copied)]
        outs = [pltpu.make_async_copy(held[i], large_out[i], out_sem.at[i]) for i in range(n_copied)]
        for copy in ins:
            copy.start()
        for i, row in enumerate(rows):
            rows_out[i][...] = vec_in[row : row + 1, :]
        for i in range(n_copied):
            ins[i].wait()
            outs[i].start()
        for copy in outs:
            copy.wait()

    return pl.pallas_call(
        kernel,
        out_shape=[jax.ShapeDtypeStruct(r.shape, r.dtype) for r in large]
        + [jax.ShapeDtypeStruct((1, share), vec.dtype) for _ in rows],
        in_specs=[hbm] * n_copied + [vmem],
        out_specs=[hbm] * n_copied + [vmem] * len(rows),
        scratch_shapes=[pltpu.VMEM(r.shape, r.dtype) for r in large]
        + [pltpu.SemaphoreType.DMA((n_copied,))] * 2,
        name="hand_on",
    )(*large, vec)


def contract_rows(left, right):
    return dot(left, right, ((0,), (0,)))


def contract_cols(left, right):
    return dot(left, right, ((1,), (1,)))


def rotary_tables(pos_ids):
    half_rot = ROT // 2
    inverse = 10000.0 ** (-(jnp.arange(half_rot, dtype=jnp.float32) * 2.0) / ROT)
    angles = pos_ids.astype(jnp.float32)[:, None] * inverse[None, :]
    cos_tab = jnp.concatenate([jnp.cos(angles), jnp.cos(angles)], axis=-1)
    sine_tab = jnp.concatenate([jnp.sin(angles), jnp.sin(angles)], axis=-1)
    return (cos_tab, sine_tab)


def rotate(blocked, cos_tab, sine_tab):
    head_part = blocked[..., :ROT]
    low_half = head_part[..., : ROT // 2]
    high_half = head_part[..., ROT // 2 :]
    turned = jnp.concatenate([-high_half, low_half], axis=-1)
    spun_part = head_part * cos_tab[:, None, :] + turned * sine_tab[:, None, :]
    return jnp.concatenate([spun_part, blocked[..., ROT:]], axis=-1)


def unrotate(grad_part, cos_tab, sine_tab):
    head_part = grad_part[..., :ROT]
    scaled = head_part * sine_tab[:, None, :]
    back_turn = jnp.concatenate([scaled[..., ROT // 2 :], -scaled[..., : ROT // 2]], axis=-1)
    return jnp.concatenate(
        [head_part * cos_tab[:, None, :] + back_turn, grad_part[..., ROT:]], axis=-1
    )


def gelu_pair(pre_act):
    cdf = 0.5 * (1.0 + lax.erf(pre_act / math.sqrt(2.0)))
    pdf = jnp.exp(-0.5 * pre_act * pre_act) / math.sqrt(2.0 * math.pi)
    return pre_act * cdf, cdf + pre_act * pdf


def normalise(rows):
    center = rows - jnp.mean(rows, axis=-1, keepdims=True)
    inv_std = lax.rsqrt(jnp.mean(center * center, axis=-1, keepdims=True) + norm_eps)
    return center * inv_std, inv_std


def heads_einsum(spec, left, right):
    return jnp.einsum(spec, left, right, preferred_element_type=jnp.float32)


def shards(
    tokens,
    segments,
    positions,
    ln1_gain,
    ln1_bias,
    ln2_gain,
    ln2_bias,
    qkv_weight,
    qkv_bias,
    dense_weight,
    dense_bias,
    fc1_weight,
    fc1_bias,
    fc2_weight,
    fc2_bias,
    cotangent,
    *,
    n_dp,
    n_t,
):
    bf16 = jnp.bfloat16
    width = tokens.shape[1]
    group = tokens.shape[0]
    share = width // n_dp
    heads_wide = qkv_weight.shape[2]
    if share % 48 == 0 and heads_wide % 128 == 64 and heads_wide % 9 == 0 and n_t == 4 and n_dp == 4 * PAIR and fc1_weight.shape[2] % 768 == 0:
        fused = fused_layer(
            (fc1_weight[0], fc2_weight[0].T, qkv_weight[0], dense_weight[0]),
            (tokens, cotangent),
            (ln1_gain, ln1_bias, ln2_gain, ln2_bias, qkv_bias, fc1_bias, dense_bias, fc2_bias),
            (segments[None, :], positions[None, :]),
            n_dp,
            n_t,
        )
        y_out, x_grad, g_up, g_down_t, g_qkv, g_dense, sum_qkv, sum_up, *owned = hand_on(
            (*fused[:6], *fused[7:9], fused[6]), 8
        )
        return (
            y_out,
            x_grad,
            *owned[:4],
            g_qkv[None],
            sum_qkv,
            g_dense[None],
            owned[4],
            g_up[None],
            sum_up,
            g_down_t.T[None],
            owned[5],
        )
    gain_a, bias_a, gain_m, bias_m = ln1_gain[0], ln1_bias[0], ln2_gain[0], ln2_bias[0]
    gathered = gather_all(
        (qkv_weight[0], dense_weight[0].T, fc1_weight[0], fc2_weight[0].T),
        (tokens, cotangent),
        n_dp,
        n_t,
    )
    w_qkv, w_dense_t, w_up, w_down_t = [g.reshape(width, -1) for g in gathered[:4]]
    seq_rows, grad_full = [g.reshape(n_t * group, width) for g in gathered[4:]]
    seq_len = seq_rows.shape[0]

    cos_tab, sine_tab = rotary_tables(positions)
    normed, _ = normalise(seq_rows.astype(jnp.float32))
    in_attn = (normed * gain_a + bias_a).astype(bf16)
    in_mlp = (normed * gain_m + bias_m).astype(bf16)

    joined = (dot(in_attn, w_qkv, ((1,), (0,))) + qkv_bias[0]).reshape(seq_len, -1, 3, HEAD_DIM)
    queries = rotate(joined[:, :, 0], cos_tab, sine_tab).astype(bf16)
    key_rows = rotate(joined[:, :, 1], cos_tab, sine_tab).astype(bf16)
    value_rows = joined[:, :, 2].astype(bf16)

    score_scale = HEAD_DIM ** (-0.5)
    places_in = jnp.arange(seq_len, dtype=jnp.int32)
    allowed = (
        (segments[:, None] == segments[None, :]) & (places_in[:, None] >= places_in[None, :])
    )[None]
    scores = heads_einsum("qhd,khd->hqk", queries, key_rows) * score_scale
    scores = jnp.where(allowed, scores, -1e30)
    row_max = jnp.max(scores, axis=-1, keepdims=True)
    row_total = jnp.sum(jnp.exp(scores - row_max), axis=-1, keepdims=True)
    log_total = row_max + jnp.log(row_total)
    prob_wide = jnp.where(allowed, jnp.exp(scores - log_total), 0.0)
    probs = prob_wide.astype(bf16)
    context = heads_einsum("hqk,khd->qhd", probs, value_rows).reshape(seq_len, -1).astype(bf16)

    pre_act = dot(in_mlp, w_up, ((1,), (0,))) + fc1_bias[0]
    hidden, slope = gelu_pair(pre_act)
    hidden = hidden.astype(bf16)
    branch = contract_cols(context, w_dense_t) + contract_cols(hidden, w_down_t)

    grad_w_dense_t = contract_rows(grad_full, context)
    grad_w_down_t = contract_rows(grad_full, hidden)
    grad_pre = dot(grad_full, w_down_t, ((1,), (0,))) * slope
    grad_b_up = jnp.sum(grad_pre, axis=0)
    grad_pre_bf = grad_pre.astype(bf16)
    grad_ctx = dot(grad_full, w_dense_t, ((1,), (0,))).astype(bf16).reshape(seq_len, -1, HEAD_DIM)
    grad_w_up = contract_rows(in_mlp, grad_pre_bf)

    grad_probs = heads_einsum("qhd,khd->hqk", grad_ctx, value_rows)
    row_dot = jnp.sum(prob_wide * grad_probs, axis=-1, keepdims=True)
    grad_scores = (prob_wide * (grad_probs - row_dot) * score_scale).astype(bf16)
    grad_q = heads_einsum("hqk,khd->qhd", grad_scores, key_rows)
    grad_k = heads_einsum("hqk,qhd->khd", grad_scores, queries)
    grad_v = heads_einsum("hqk,qhd->khd", probs, grad_ctx)
    grad_joined = jnp.stack(
        [unrotate(grad_q, cos_tab, sine_tab), unrotate(grad_k, cos_tab, sine_tab), grad_v], axis=2
    ).reshape(seq_len, -1)
    grad_b_qkv = jnp.sum(grad_joined, axis=0)
    grad_joined_bf = grad_joined.astype(bf16)
    grad_w_qkv = contract_rows(in_attn, grad_joined_bf)

    part_attn = contract_cols(grad_joined_bf, w_qkv)
    part_mlp = contract_cols(grad_pre_bf, w_up)
    grad_rows = cotangent.astype(jnp.float32)
    heads_wide = grad_b_qkv.shape[0]
    n_vec = max(width, heads_wide, grad_b_up.shape[0])

    def lane(v):
        return jnp.pad(v, (0, n_vec - v.shape[0]))

    vec = jnp.stack(
        [
            lane(jnp.sum(part_attn * normed, axis=0)),
            lane(jnp.sum(part_attn, axis=0)),
            lane(jnp.sum(part_mlp * normed, axis=0)),
            lane(jnp.sum(part_mlp, axis=0)),
            lane(jnp.sum(grad_rows, axis=0)),
            lane(grad_b_qkv),
            lane(grad_b_up),
            jnp.zeros((n_vec,), jnp.float32),
        ]
    )

    def blocks(grad):
        return grad.astype(bf16).reshape(n_dp, width // n_dp, -1)

    def groups(part):
        return part.astype(bf16).reshape(n_t, group, width)

    (g_qkv, g_dense_t, g_up, g_down_t, mixed, grad_in_attn, grad_in_mlp, vec_sums) = reduce_all(
        (blocks(grad_w_qkv), blocks(grad_w_dense_t), blocks(grad_w_up), blocks(grad_w_down_t)),
        (groups(branch), groups(part_attn), groups(part_mlp)),
        vec,
        n_dp,
        n_t,
    )

    own_rows = tokens.astype(jnp.float32)
    own_normed, inv_std = normalise(own_rows)
    y_out = own_rows + mixed + dense_bias[0] + fc2_bias[0]
    grad_normed = grad_in_attn * gain_a + grad_in_mlp * gain_m
    x_grad = grad_rows + inv_std * (
        grad_normed
        - jnp.mean(grad_normed, axis=-1, keepdims=True)
        - own_normed * jnp.mean(grad_normed * own_normed, axis=-1, keepdims=True)
    )
    share = width // n_dp
    owned = lax.dynamic_slice_in_dim(vec_sums[1], lax.axis_index("dp") * share, share, axis=1)
    return (
        y_out,
        x_grad,
        owned[0:1],
        owned[1:2],
        owned[2:3],
        owned[3:4],
        g_qkv[None],
        vec_sums[0, 5:6, :heads_wide],
        g_dense_t.T[None],
        owned[4:5],
        g_up[None],
        vec_sums[0, 6:7, : grad_b_up.shape[0]],
        g_down_t.T[None],
        owned[4:5],
    )


def solution(mesh):
    placed = (
        P(("dp", "tensor"), None),
        P("dp"),
        P("dp"),
        P(),
        P(),
        P(),
        P(),
        P(None, "dp", "tensor"),
        P(None, "tensor"),
        P(None, "tensor", "dp"),
        P(),
        P(None, "dp", "tensor"),
        P(None, "tensor"),
        P(None, "tensor", "dp"),
        P(),
        P(("dp", "tensor"), None),
    )

    def step(*args):
        return shards(*args, n_dp=mesh.shape["dp"], n_t=mesh.shape["tensor"])

    return jax.shard_map(
        step,
        mesh=mesh,
        in_specs=placed,
        out_specs=(
            P(("dp", "tensor"), None),
            P(("dp", "tensor"), None),
            P(None, "dp"),
            P(None, "dp"),
            P(None, "dp"),
            P(None, "dp"),
            P(None, "dp", "tensor"),
            P(None, "tensor"),
            P(None, "tensor", "dp"),
            P(None, "dp"),
            P(None, "dp", "tensor"),
            P(None, "tensor"),
            P(None, "tensor", "dp"),
            P(None, "dp"),
        ),
        check_vma=False,
    )
```

```python
import math

import jax
import jax.numpy as jnp
from jax import lax
from jax.experimental import pallas as pl
from jax.experimental.pallas import tpu as pltpu
from jax.sharding import PartitionSpec as P

HEAD_DIM = 64
ROT = 16
PAIR = 2
MESH = pl.DeviceIdType.MESH

norm_eps = 1e-05


def places(n_dp, n_t):
    dp = lax.axis_index("dp")
    t = lax.axis_index("tensor")
    return dp, t, dp // PAIR, lax.rem(dp, PAIR), n_dp // PAIR


def greet(devices):
    barrier = pltpu.get_barrier_semaphore()
    for device, there in devices:
        if there is None:
            pl.semaphore_signal(barrier, inc=1, device_id=device, device_id_type=MESH)
        else:

            @pl.when(there)
            def _(device=device):
                pl.semaphore_signal(barrier, inc=1, device_id=device, device_id_type=MESH)

    expected = sum(1 if there is None else there.astype(jnp.int32) for _, there in devices)
    pl.semaphore_wait(barrier, expected)


def gather_kernel(n_dp, n_t, n_w, *refs):
    w_in = refs[:n_w]
    rows_in = refs[n_w : n_w + 2]
    w_out = refs[n_w + 2 : 2 * n_w + 2]
    rows_out = refs[2 * n_w + 2 : 2 * n_w + 4]
    r_send, r_recv, l_send, l_recv, y_send, y_recv, t_send, t_recv = refs[2 * n_w + 4 :]
    dp, t, z, y, height = places(n_dp, n_t)
    mate = (z * PAIR + (1 - y), t)
    right = (jnp.minimum(z + 1, height - 1) * PAIR + y, t)
    left = (jnp.maximum(z - 1, 0) * PAIR + y, t)
    has_right = z + 1 < height
    has_left = z >= 1
    greet(
        [(mate, None), (right, has_right), (left, has_left)]
        + [((dp, lax.rem(t + k, n_t)), None) for k in range(1, n_t)]
    )

    def line(src, a, block, step, send, recv, device):
        return pltpu.make_async_remote_copy(
            src_ref=src,
            dst_ref=w_out[a].at[block * PAIR + y],
            send_sem=send.at[a, step],
            recv_sem=recv.at[a, step],
            device_id=device,
            device_id_type=MESH,
        )

    def across(src, a, block, side):
        return pltpu.make_async_remote_copy(
            src_ref=src,
            dst_ref=w_out[a].at[block * PAIR + side],
            send_sem=y_send.at[a, block],
            recv_sem=y_recv.at[a, block],
            device_id=mate,
            device_id_type=MESH,
        )

    def peer_copy(i, k, owner):
        return pltpu.make_async_remote_copy(
            src_ref=rows_in[i],
            dst_ref=rows_out[i].at[owner],
            send_sem=t_send.at[i, k - 1],
            recv_sem=t_recv.at[i, k - 1],
            device_id=(dp, lax.rem(t + k, n_t)),
            device_id_type=MESH,
        )

    for a in range(n_w):

        @pl.when(has_right)
        def _(a=a):
            line(w_in[a], a, z, 0, r_send, r_recv, right).start()

        @pl.when(has_left)
        def _(a=a):
            line(w_in[a], a, z, 0, l_send, l_recv, left).start()

        across(w_in[a], a, z, y).start()
    for i in range(2):
        for k in range(1, n_t):
            peer_copy(i, k, t).start()
    for a in range(n_w):
        w_out[a][dp] = w_in[a][...]
    for i in range(2):
        rows_out[i][t] = rows_in[i][...]

    for step in range(height - 1):
        for a in range(n_w):
            from_left = z - 1 - step
            from_right = z + 1 + step

            @pl.when(from_left >= 0)
            def _(a=a, block=from_left, step=step):
                held = w_out[a].at[block * PAIR + y]
                line(held, a, block, step, r_send, r_recv, right).wait_recv()
                across(held, a, block, y).start()
                if step + 1 < height - 1:

                    @pl.when(has_right)
                    def _():
                        line(held, a, block, step + 1, r_send, r_recv, right).start()

            @pl.when(from_right < height)
            def _(a=a, block=from_right, step=step):
                held = w_out[a].at[block * PAIR + y]
                line(held, a, block, step, l_send, l_recv, left).wait_recv()
                across(held, a, block, y).start()
                if step + 1 < height - 1:

                    @pl.when(has_left)
                    def _():
                        line(held, a, block, step + 1, l_send, l_recv, left).start()

    for i in range(2):
        for k in range(1, n_t):
            peer_copy(i, k, lax.rem(t + n_t - k, n_t)).wait_recv()
            peer_copy(i, k, t).wait_send()
    for a in range(n_w):
        for step in range(height - 1):

            @pl.when((z - step >= 0) & has_right)
            def _(a=a, step=step):
                line(w_in[a], a, z, step, r_send, r_recv, right).wait_send()

            @pl.when((z + step < height) & has_left)
            def _(a=a, step=step):
                line(w_in[a], a, z, step, l_send, l_recv, left).wait_send()

        for block in range(height):
            across(w_in[a], a, block, y).wait_send()
            across(w_in[a], a, block, 1 - y).wait_recv()


def gather_all(weights, rows, n_dp, n_t):
    n_w = len(weights)
    height = n_dp // PAIR
    vmem = pl.BlockSpec(memory_space=pltpu.VMEM)
    dma = pltpu.SemaphoreType.DMA

    def kernel(*refs):
        gather_kernel(n_dp, n_t, n_w, *refs)

    return pl.pallas_call(
        kernel,
        out_shape=[jax.ShapeDtypeStruct((n_dp,) + w.shape, w.dtype) for w in weights]
        + [jax.ShapeDtypeStruct((n_t,) + r.shape, r.dtype) for r in rows],
        in_specs=[vmem] * (n_w + 2),
        out_specs=[vmem] * (n_w + 2),
        scratch_shapes=[
            dma((n_w, height - 1)),
            dma((n_w, height - 1)),
            dma((n_w, height - 1)),
            dma((n_w, height - 1)),
            dma((n_w, height)),
            dma((n_w, height)),
            dma((2, n_t - 1)),
            dma((2, n_t - 1)),
        ],
        compiler_params=pltpu.CompilerParams(collective_id=0, has_side_effects=True),
        name="gather_all",
    )(*weights, *rows)


def reduce_kernel(n_dp, n_t, n_w, n_r, *refs):
    g_in = refs[:n_w]
    p_in = refs[n_w : n_w + n_r]
    vec_in = refs[n_w + n_r]
    base = n_w + n_r + 1
    g_out = refs[base : base + n_w]
    p_out = refs[base + n_w : base + n_w + n_r]
    vec_out = refs[base + n_w + n_r]
    base = 2 * base
    y_buf = refs[base : base + n_w]
    s_buf = refs[base + n_w : base + 2 * n_w]
    z_buf = refs[base + 2 * n_w : base + 3 * n_w]
    base += 3 * n_w
    p_buf = refs[base : base + n_r]
    vy_buf, vs_buf, vz_buf, vd_buf, vt_buf = refs[base + n_r : base + n_r + 5]
    (
        y_send,
        y_recv,
        z_send,
        z_recv,
        p_send,
        p_recv,
        v_send,
        v_recv,
    ) = refs[base + n_r + 5 :]
    dp, t, z, y, height = places(n_dp, n_t)
    mate = (z * PAIR + (1 - y), t)

    def at_z(k):
        return lax.rem(z + k, height)

    greet(
        [(mate, None)]
        + [((at_z(k) * PAIR + y, t), None) for k in range(1, height)]
        + [((dp, lax.rem(t + k, n_t)), None) for k in range(1, n_t)]
    )

    def remote(src, dst, send, recv, device):
        return pltpu.make_async_remote_copy(
            src_ref=src,
            dst_ref=dst,
            send_sem=send,
            recv_sem=recv,
            device_id=device,
            device_id_type=MESH,
        )

    order = [k for k in range(1, height)] + [0]

    def swap(a, k):
        return remote(
            g_in[a].at[at_z(k) * PAIR + (1 - y)],
            y_buf[a].at[k],
            y_send.at[a, k],
            y_recv.at[a, k],
            mate,
        )

    def to_owner(a, k):
        return remote(
            s_buf[a].at[k - 1],
            z_buf[a].at[k - 1],
            z_send.at[a, k - 1],
            z_recv.at[a, k - 1],
            (at_z(k) * PAIR + y, t),
        )

    def to_peer(i, k):
        return remote(
            p_in[i].at[lax.rem(t + k, n_t)],
            p_buf[i].at[k - 1],
            p_send.at[i, k - 1],
            p_recv.at[i, k - 1],
            (dp, lax.rem(t + k, n_t)),
        )

    vec_swap = remote(vec_in, vy_buf, v_send.at[0], v_recv.at[0], mate)

    def vec_owner(k):
        return remote(
            vs_buf, vz_buf.at[k - 1], v_send.at[k], v_recv.at[k], (at_z(k) * PAIR + y, t)
        )

    def vec_peer(k):
        at = height - 1 + k
        return remote(
            vd_buf, vt_buf.at[k - 1], v_send.at[at], v_recv.at[at], (dp, lax.rem(t + k, n_t))
        )

    vec_swap.start()
    for k in order:
        for a in range(n_w):
            swap(a, k).start()
    for i in range(n_r):
        for k in range(1, n_t):
            to_peer(i, k).start()

    vec_swap.wait_recv()
    vs_buf[...] = vec_in[...] + vy_buf[...]
    for k in range(1, height):
        vec_owner(k).start()

    for k in range(1, height):
        for a in range(n_w):
            swap(a, k).wait_recv()
            own = g_in[a][at_z(k) * PAIR + y].astype(jnp.float32)
            s_buf[a][k - 1] = (own + y_buf[a][k].astype(jnp.float32)).astype(jnp.bfloat16)
            to_owner(a, k).start()
        if k == 1:
            total = vs_buf[...]
            for j in range(1, height):
                vec_owner(j).wait_recv()
                total = total + vz_buf[j - 1]
            vd_buf[...] = total
            for j in range(1, n_t):
                vec_peer(j).start()

    for i in range(n_r):
        total = p_in[i][t].astype(jnp.float32)
        for k in range(1, n_t):
            to_peer(i, k).wait_recv()
            total = total + p_buf[i][k - 1].astype(jnp.float32)
        p_out[i][...] = total

    total = vd_buf[...]
    for k in range(1, n_t):
        vec_peer(k).wait_recv()
        total = total + vt_buf[k - 1]
    vec_out[0] = vd_buf[...]
    vec_out[1] = total

    for a in range(n_w):
        swap(a, 0).wait_recv()
        total = g_in[a][dp].astype(jnp.float32) + y_buf[a][0].astype(jnp.float32)
        g_out[a][...] = total
    for k in range(1, height):
        for a in range(n_w):
            to_owner(a, k).wait_recv()
            g_out[a][...] += z_buf[a][k - 1].astype(jnp.float32)

    vec_swap.wait_send()
    for k in range(1, height):
        vec_owner(k).wait_send()
    for k in range(1, n_t):
        vec_peer(k).wait_send()
    for a in range(n_w):
        for k in range(height):
            swap(a, k).wait_send()
        for k in range(1, height):
            to_owner(a, k).wait_send()
    for i in range(n_r):
        for k in range(1, n_t):
            to_peer(i, k).wait_send()


def reduce_all(grads, parts, vec, n_dp, n_t):
    n_w, n_r = len(grads), len(parts)
    height = n_dp // PAIR
    vmem = pl.BlockSpec(memory_space=pltpu.VMEM)
    dma = pltpu.SemaphoreType.DMA

    def kernel(*refs):
        reduce_kernel(n_dp, n_t, n_w, n_r, *refs)

    n_in = n_w + n_r + 1
    n_vec = height + n_t - 1
    return pl.pallas_call(
        kernel,
        out_shape=[jax.ShapeDtypeStruct(g.shape[1:], jnp.float32) for g in grads]
        + [jax.ShapeDtypeStruct(p.shape[1:], jnp.float32) for p in parts]
        + [jax.ShapeDtypeStruct((2,) + vec.shape, jnp.float32)],
        in_specs=[vmem] * n_in,
        out_specs=[vmem] * n_in,
        scratch_shapes=[pltpu.VMEM((height,) + g.shape[1:], jnp.bfloat16) for g in grads]
        + [pltpu.VMEM((height - 1,) + g.shape[1:], jnp.bfloat16) for g in grads]
        + [pltpu.VMEM((height - 1,) + g.shape[1:], jnp.bfloat16) for g in grads]
        + [pltpu.VMEM((n_t - 1,) + p.shape[1:], jnp.bfloat16) for p in parts]
        + [
            pltpu.VMEM(vec.shape, jnp.float32),
            pltpu.VMEM(vec.shape, jnp.float32),
            pltpu.VMEM((height - 1,) + vec.shape, jnp.float32),
            pltpu.VMEM(vec.shape, jnp.float32),
            pltpu.VMEM((n_t - 1,) + vec.shape, jnp.float32),
        ]
        + [
            dma((n_w, height)),
            dma((n_w, height)),
            dma((n_w, height - 1)),
            dma((n_w, height - 1)),
            dma((n_r, n_t - 1)),
            dma((n_r, n_t - 1)),
            dma((n_vec,)),
            dma((n_vec,)),
        ],
        compiler_params=pltpu.CompilerParams(collective_id=1, has_side_effects=True),
        name="reduce_all",
    )(*grads, *parts, vec)


def dot(left, right, dims):
    return lax.dot_general(left, right, (dims, ((), ())), preferred_element_type=jnp.float32)


NN = ((1,), (0,))
NT = ((1,), (1,))
TN = ((0,), (0,))


def fused_kernel(n_dp, n_t, cuts, extra, refs):
    bf16, f32 = jnp.bfloat16, jnp.float32
    (
        w_up_in,
        w_down_in,
        w_qkv_in,
        w_dense_in,
        tok_in,
        cot_in,
        gain_a,
        bias_a,
        gain_m,
        bias_m,
        b_qkv,
        b_up,
        b_dense,
        b_down,
        seg_row,
        pos_row,
        y_ref,
        x_ref,
        g_up,
        g_down,
        g_qkv,
        g_dense,
        vec_out,
        qkv_bias_out,
        up_bias_out,
    ) = refs[:25]
    rest = list(refs[25:])

    def take(n):
        got = rest[:n]
        del rest[:n]
        return got

    n_p = 1 + 2 * (len(cuts) - 1)
    w_all, g_in, y_buf, s_buf, z_buf = take(n_p), take(n_p), take(n_p), take(n_p), take(n_p)
    half_buf = take(n_p)
    rows_all, p_in, pc_buf, px_out, px_buf = take(2), take(3), take(3), take(3), take(3)
    vec_in, vy_buf, vs_buf, vz_buf, vd_buf, vt_buf = take(6)
    normed, in_a, in_m, in_at, in_mt, grad_t, hidden, grad_pre, joined, cos_w, sin_a, sin_b = take(12)
    w_att, g_att = take(2)
    r_send, r_recv, l_send, l_recv, rb_send, rb_recv, lb_send, lb_recv, f_send, f_recv = take(10)
    y_send, y_recv, z_send, z_recv, h_recv = take(5)
    t_send, t_recv, p_send, p_recv, v_send, v_recv = take(6)

    dp, t, z, y, height = places(n_dp, n_t)
    group, width = tok_in.shape
    share = w_up_in.shape[0]
    near = share - extra
    seq = group * n_t
    wide = joined.shape[1]
    heads_wide = w_qkv_in.shape[1]
    n_heads = heads_wide // (3 * HEAD_DIM)
    mate = (z * PAIR + (1 - y), t)
    right = (jnp.minimum(z + 1, height - 1) * PAIR + y, t)
    left = (jnp.maximum(z - 1, 0) * PAIR + y, t)
    has_right = z + 1 < height
    has_left = z >= 1
    side, core = t // 2, lax.rem(t, 2)
    twin = (dp, side * 2 + (1 - core))
    over = (dp, (1 - side) * 2 + core)

    def at_z(k):
        return lax.rem(z + k, height)

    def z_device(k):
        return (at_z(k) * PAIR + y, t)

    def t_device(k):
        return (dp, lax.rem(t + k, n_t))

    greet(
        [(mate, None)]
        + [(z_device(k), None) for k in range(1, height)]
        + [(t_device(k), None) for k in range(1, n_t)]
    )

    def remote(src, dst, send, recv, device):
        return pltpu.make_async_remote_copy(
            src_ref=src,
            dst_ref=dst,
            send_sem=send,
            recv_sem=recv,
            device_id=device,
            device_id_type=MESH,
        )

    n_c = len(cuts) - 1
    w_in = [w_att]
    g_out = [g_att]
    for c in range(n_c):
        at = pl.ds(cuts[c], cuts[c + 1] - cuts[c])
        w_in += [w_up_in.at[:, at], w_down_in.at[:, at]]
        g_out += [g_up.at[:, at], g_down.at[:, at]]
    attn = (0,)
    chunk = [(1 + 2 * c, 2 + 2 * c) for c in range(n_c)]
    low_part = heads_wide // 128 * 128
    shift = heads_wide - low_part
    all_wide = w_att.shape[1]
    everything = tuple(range(n_p))

    tail_rows = pl.ds(near, extra)
    near_rows = pl.ds(0, near)

    def line(src, a, block, step, send, recv, device):
        return remote(
            src, w_all[a].at[block * PAIR + y], send.at[a, step], recv.at[a, step], device
        )

    def line_b(a, block, step, send, recv, device):
        held = w_all[a].at[block * PAIR + (1 - y), tail_rows]
        return remote(held, held, send.at[a, step], recv.at[a, step], device)

    def across_own(a, at):
        return remote(
            w_in[a], w_all[a].at[z * PAIR + at], f_send.at[a, z], f_recv.at[a, z], mate
        )

    def across(a, block, at):
        held = w_all[a].at[block * PAIR + at, near_rows]
        return remote(held, held, f_send.at[a, block], f_recv.at[a, block], mate)

    def send_own(arrays):
        for a in arrays:

            @pl.when(has_right)
            def _(a=a):
                line(w_in[a], a, z, 0, r_send, r_recv, right).start()

            @pl.when(has_left)
            def _(a=a):
                line(w_in[a], a, z, 0, l_send, l_recv, left).start()

            across_own(a, y).start()

    def send_mates(arrays):
        for a in arrays:
            across_own(a, 1 - y).wait_recv()

            @pl.when(has_right)
            def _(a=a):
                line_b(a, z, 0, rb_send, rb_recv, right).start()

            @pl.when(has_left)
            def _(a=a):
                line_b(a, z, 0, lb_send, lb_recv, left).start()

    def relay(step, arrays):
        for a in arrays:
            from_left = z - 1 - step
            from_right = z + 1 + step

            @pl.when(from_left >= 0)
            def _(a=a, block=from_left):
                held = w_all[a].at[block * PAIR + y]
                line(held, a, block, step, r_send, r_recv, right).wait_recv()
                if step + 1 < height - 1:

                    @pl.when(has_right)
                    def _():
                        line(held, a, block, step + 1, r_send, r_recv, right).start()

                across(a, block, y).start()

            @pl.when(from_right < height)
            def _(a=a, block=from_right):
                held = w_all[a].at[block * PAIR + y]
                line(held, a, block, step, l_send, l_recv, left).wait_recv()
                if step + 1 < height - 1:

                    @pl.when(has_left)
                    def _():
                        line(held, a, block, step + 1, l_send, l_recv, left).start()

                across(a, block, y).start()

        for a in arrays:

            @pl.when(z - 1 - step >= 0)
            def _(a=a, block=z - 1 - step):
                line_b(a, block, step, rb_send, rb_recv, right).wait_recv()
                if step + 1 < height - 1:

                    @pl.when(has_right)
                    def _():
                        line_b(a, block, step + 1, rb_send, rb_recv, right).start()

            @pl.when(z + 1 + step < height)
            def _(a=a, block=z + 1 + step):
                line_b(a, block, step, lb_send, lb_recv, left).wait_recv()
                if step + 1 < height - 1:

                    @pl.when(has_left)
                    def _():
                        line_b(a, block, step + 1, lb_send, lb_recv, left).start()

    def land(arrays):
        for a in arrays:
            for block in range(height):

                @pl.when(z != block)
                def _(a=a, block=block):
                    across(a, block, 1 - y).wait_recv()

    rows_in = (tok_in, cot_in)

    def row_copy(src, i, k, owner, device):
        return remote(src, rows_all[i].at[owner], t_send.at[i, k], t_recv.at[i, k], device)

    below = 1 - z // 2
    at_end = lax.rem(z // 2 + z + 1, 2)
    opposite, across_mid = 3 * below, 1 + below
    beside = below * (1 - z) + (1 - below) * (5 - z)
    inner = below * 1 + (1 - below) * 2
    owners = (
        at_end * opposite + (1 - at_end) * beside,
        at_end * across_mid + (1 - at_end) * opposite,
        at_end * beside + (1 - at_end) * across_mid,
        z,
    )

    def swap(a, k):
        return remote(
            g_in[a].at[owners[k] * PAIR + (1 - y)],
            y_buf[a].at[k],
            y_send.at[a, k],
            y_recv.at[a, k],
            mate,
        )

    def to_half(a, k):
        return remote(
            s_buf[a].at[k],
            half_buf[a].at[k],
            z_send.at[a, k],
            h_recv.at[a, k],
            (inner * PAIR + y, t),
        )

    def to_owner(a, k, slot):
        return remote(
            s_buf[a].at[k],
            z_buf[a].at[slot],
            z_send.at[a, k],
            z_recv.at[a, slot],
            (owners[k] * PAIR + y, t),
        )

    turns = (0, 1, 2, 3)

    def swap_all(arrays):
        for k in turns:
            for a in arrays:
                swap(a, k).start()

    def wide_of(ref, *at):
        return ref[at].astype(f32)

    def settle(arrays, k):
        for a in arrays:
            swap(a, k).wait_recv()
            pair = wide_of(g_in[a], owners[k] * PAIR + y) + wide_of(y_buf[a], k)

            @pl.when(at_end == 1)
            def _(a=a, pair=pair):
                s_buf[a][k] = pair.astype(bf16)
                if k < 2:
                    to_half(a, k).start()
                else:
                    to_owner(a, k, 1).start()

            @pl.when(at_end == 0)
            def _(a=a, pair=pair):
                if k == 0:
                    s_buf[a][k] = pair.astype(bf16)
                    to_owner(a, k, 1).start()
                else:
                    to_half(a, k - 1).wait_recv()
                    s_buf[a][k] = (pair + wide_of(half_buf[a], k - 1)).astype(bf16)
                    to_owner(a, k, 0).start()

    def close(arrays):
        for a in arrays:
            swap(a, 3).wait_recv()
            total = wide_of(g_in[a], dp) + wide_of(y_buf[a], 3)
            for slot in range(2):
                to_owner(a, 0, slot).wait_recv()
                total = total + wide_of(z_buf[a], slot)
            g_out[a][...] = total

    def to_twin(i):
        return remote(p_in[i].at[1 - core], pc_buf[i], p_send.at[i, 0], p_recv.at[i, 0], twin)

    def to_over(i):
        return remote(px_out[i], px_buf[i], p_send.at[i, 1], p_recv.at[i, 1], over)

    def part_over(i):
        to_twin(i).wait_recv()
        px_out[i][...] = (
            wide_of(p_in[i], core, 1 - side) + wide_of(pc_buf[i], 1 - side)
        ).astype(bf16)
        to_over(i).start()

    def part_sum(i):
        to_over(i).wait_recv()
        return wide_of(p_in[i], core, side) + wide_of(pc_buf[i], side) + px_buf[i][...].astype(f32)

    vec_swap = remote(vec_in, vy_buf, v_send.at[0], v_recv.at[0], mate)

    def vec_owner(k):
        return remote(vs_buf, vz_buf.at[k - 1], v_send.at[k], v_recv.at[k], z_device(k))

    def vec_peer(k):
        at = height - 1 + k
        return remote(vd_buf, vt_buf.at[k - 1], v_send.at[at], v_recv.at[at], t_device(k))

    w_att[:, low_part:] = jnp.concatenate(
        [jnp.zeros((shift, share), bf16), w_dense_in[...]], axis=0
    ).T
    w_att[:, :heads_wide] = w_qkv_in[...]
    send_own(attn)
    for i in range(2):
        row_copy(rows_in[i], i, 0, t, over).start()
        row_copy(rows_in[i], i, 1, t, twin).start()
    for i in range(2):
        rows_all[i][t] = rows_in[i][...]
    for a in everything:
        w_all[a][dp] = w_in[a][...]

    send_own(chunk[0])
    send_mates(attn)
    relay(0, attn)

    lanes = lax.broadcasted_iota(jnp.int32, (8, wide), 1)
    subs = lax.broadcasted_iota(jnp.int32, (8, wide), 0)
    part = lax.rem(lanes, HEAD_DIM)
    kind = lax.rem(lanes // HEAD_DIM, 3)
    turning = (kind < 2) & (lanes < heads_wide)
    low = (turning & (part == subs)).astype(f32)
    high = (turning & (part == subs + ROT // 2)).astype(f32)
    still = 1.0 - jnp.sum(low + high, axis=0, keepdims=True)

    def spread(table, where):
        return lax.dot_general(
            table, where, (TN, ((), ())), preferred_element_type=f32, precision=lax.Precision.HIGHEST
        )

    half_rot = ROT // 2
    order = lax.broadcasted_iota(jnp.int32, (half_rot, seq), 0)
    inverse = jnp.zeros((half_rot, seq), f32)
    for i in range(half_rot):
        inverse = jnp.where(order == i, 10000.0 ** (-2.0 * i / ROT), inverse)
    angles = pos_row[...].astype(f32) * inverse
    cos8, sin8 = jnp.cos(angles), jnp.sin(angles)
    cos_w[...] = spread(cos8, low + high) + still
    sin_a[...] = -spread(sin8, low)
    sin_b[...] = spread(sin8, high)

    far = (1 - side) * 2
    for i in range(2):
        row_copy(rows_in[i], i, 0, far + core, over).wait_recv()
        row_copy(rows_all[i].at[far + core], i, 2, far + core, twin).start()
        if i == 0:
            relay(1, attn)
            send_mates(chunk[0])
    for i in range(2):
        row_copy(rows_in[i], i, 1, side * 2 + (1 - core), twin).wait_recv()
        row_copy(rows_in[i], i, 2, far + (1 - core), twin).wait_recv()

    def norm_of(rows):
        center = rows - jnp.mean(rows, axis=-1, keepdims=True)
        inv_std = lax.rsqrt(jnp.mean(center * center, axis=-1, keepdims=True) + norm_eps)
        return center * inv_std, inv_std

    for g in range(n_t):
        at = pl.ds(g * group, group)
        value, _ = norm_of(rows_all[0][g].astype(f32))
        normed[at, :] = value
        va = (value * gain_a[...] + bias_a[...]).astype(bf16)
        vm = (value * gain_m[...] + bias_m[...]).astype(bf16)
        in_a[at, :] = va
        in_m[at, :] = vm
        in_at[:, at] = va.T
        in_mt[:, at] = vm.T
        grad_t[:, at] = rows_all[1][g].T
        if g == 0:
            relay(2, attn)
            send_own(chunk[1])
    grad_full = rows_all[1][...].reshape(seq, width)
    land(attn)

    def blocks(grad):
        return grad.astype(bf16).reshape(n_dp, share, -1)

    def whole(a):
        return w_all[a][...].reshape(width, -1)

    vec_in[...] = jnp.zeros_like(vec_in)
    w_qkv = w_all[0][:, :, :wide].reshape(width, -1)
    w_dense = w_all[0][:, :, low_part:].reshape(width, -1)
    joined[...] = dot(in_a[...], w_qkv, NN)
    joined[:, :heads_wide] += b_qkv[...]
    joined[:, heads_wide:] = jnp.zeros((seq, wide - heads_wide), f32)

    def turn(value, sign):
        moved = pltpu.roll(value, wide - ROT // 2, 1) * sin_a[...]
        moved = moved + pltpu.roll(value, ROT // 2, 1) * sin_b[...]
        return value * cos_w[...] + sign * moved

    relay(0, chunk[0])
    turned = turn(joined[...], 1.0).astype(bf16)
    grad_ctx = dot(grad_full, w_dense, NN).astype(bf16)
    row_at = lax.broadcasted_iota(jnp.int32, (seq, seq), 0)
    col_at = lax.broadcasted_iota(jnp.int32, (seq, seq), 1)
    seg_at = seg_row[...].astype(f32)
    seg_col = jnp.broadcast_to(seg_at, (128, seq)).T[:, :1]
    allowed = (seg_col == seg_at) & (row_at >= col_at)
    scale = HEAD_DIM ** (-0.5)
    contexts = [jnp.zeros((seq, shift), bf16)]
    for h in range(n_heads):
        base = h * 3 * HEAD_DIM
        q = turned[:, base : base + HEAD_DIM]
        k_h = turned[:, base + HEAD_DIM : base + 2 * HEAD_DIM]
        v = turned[:, base + 2 * HEAD_DIM : base + 3 * HEAD_DIM]
        gc = grad_ctx[:, shift + h * HEAD_DIM : shift + (h + 1) * HEAD_DIM]
        scores = jnp.where(allowed, dot(q, k_h, NT) * scale, -1e30)
        e = jnp.exp(scores - jnp.max(scores, axis=-1, keepdims=True))
        p = e * (1.0 / jnp.sum(e, axis=-1, keepdims=True))
        pb = p.astype(bf16)
        contexts.append(dot(pb, v, NN).astype(bf16))
        gp = dot(gc, v, NT)
        row_dot = jnp.sum(p * gp, axis=-1, keepdims=True)
        gs = (p * (gp - row_dot) * scale).astype(bf16)
        joined[:, base : base + HEAD_DIM] = dot(gs, k_h, NN)
        joined[:, base + HEAD_DIM : base + 2 * HEAD_DIM] = dot(gs, q, TN)
        joined[:, base + 2 * HEAD_DIM : base + 3 * HEAD_DIM] = dot(pb, gc, TN)
        if h == 0:
            send_mates(chunk[1])
        if h == 1:
            relay(1, chunk[0])
    context = jnp.concatenate(contexts, axis=1)
    grad_joined = turn(joined[...], -1.0)
    vec_in[5:6, :wide] = jnp.sum(grad_joined, axis=0, keepdims=True)
    gj = grad_joined.astype(bf16)
    for_qkv = dot(in_at[...], gj, NN)
    for_dense = dot(grad_t[...], context, NN)
    g_in[0][:, :, :low_part] = blocks(for_qkv[:, :low_part])
    g_in[0][:, :, low_part:wide] = blocks(for_qkv[:, low_part:] + for_dense[:, : wide - low_part])
    g_in[0][:, :, wide:] = blocks(for_dense[:, wide - low_part :])
    swap_all(attn)
    relay(2, chunk[0])
    relay(0, chunk[1])

    def feed(c, g):
        at = pl.ds(g * group, group)
        cols = pl.ds(cuts[c], cuts[c + 1] - cuts[c])
        up, down = chunk[c]
        pre = dot(in_m[at, :], whole(up), NN) + b_up[:, cols]
        cdf = 0.5 * (1.0 + lax.erf(pre / math.sqrt(2.0)))
        pdf = jnp.exp(-0.5 * pre * pre) / math.sqrt(2.0 * math.pi)
        hidden[at, cols] = (pre * cdf).astype(bf16)
        gp = dot(rows_all[1][g], whole(down), NN) * (cdf + pre * pdf)
        vec_in[6:7, cols] += jnp.sum(gp, axis=0, keepdims=True)
        grad_pre[at, cols] = gp.astype(bf16)

    def feed_grads(c):
        cols = pl.ds(cuts[c], cuts[c + 1] - cuts[c])
        up, down = chunk[c]
        g_in[up][...] = blocks(dot(in_mt[...], grad_pre[:, cols], NN))
        swap_all((up,))
        g_in[down][...] = blocks(dot(grad_t[...], hidden[:, cols], NN))
        swap_all((down,))

    def units(c):
        return pl.ds(cuts[c], cuts[c + 1] - cuts[c])

    land(chunk[0])
    for g in range(n_t):
        feed(0, g)
        if g == 1:
            relay(1, chunk[1])
    relay(2, chunk[1])
    feed_grads(0)
    settle(attn, turns[0])
    for g in range(n_t):
        at = pl.ds(g * group, group)
        pa = dot(gj[g * group : (g + 1) * group], w_qkv, NT)
        vec_in[0:1, :width] += jnp.sum(pa * normed[at, :], axis=0, keepdims=True)
        vec_in[1:2, :width] += jnp.sum(pa, axis=0, keepdims=True)
        p_in[1][g % 2, g // 2] = pa.astype(bf16)
    to_twin(1).start()
    settle(attn, turns[1])
    grad_rows = cot_in[...].astype(f32)
    vec_in[4:5, :width] = jnp.sum(grad_rows, axis=0, keepdims=True)
    land(chunk[1])
    for g in range(n_t):
        feed(1, g)
        if g == 1:
            settle(attn, turns[2])
    part_over(1)
    for g in range(n_t):
        at = pl.ds(g * group, group)
        pm = dot(grad_pre[at, units(0)], whole(chunk[0][0]), NT)
        for c in range(1, n_c):
            pm = pm + dot(grad_pre[at, units(c)], whole(chunk[c][0]), NT)
        vec_in[2:3, :width] += jnp.sum(pm * normed[at, :], axis=0, keepdims=True)
        vec_in[3:4, :width] += jnp.sum(pm, axis=0, keepdims=True)
        p_in[2][g % 2, g // 2] = pm.astype(bf16)
    vec_swap.start()
    to_twin(2).start()
    feed_grads(1)
    for k in turns[:2]:
        settle(chunk[0][:1], k)
    for g in range(n_t):
        at = pl.ds(g * group, group)
        branch = dot(context[g * group : (g + 1) * group], w_dense, NT)
        for c in range(n_c):
            branch = branch + dot(hidden[at, units(c)], whole(chunk[c][1]), NT)
        p_in[0][g % 2, g // 2] = branch.astype(bf16)
    to_twin(0).start()
    settle(chunk[0][:1], turns[2])
    part_over(2)
    settle(chunk[0][1:], turns[0])
    part_over(0)
    settle(chunk[0][1:], turns[1])
    close(attn)
    g_qkv[...] = g_att[:, :heads_wide]
    g_dense[...] = g_att[:, low_part:].T[shift:]
    settle(chunk[0][1:], turns[2])
    vec_swap.wait_recv()
    vs_buf[...] = vec_in[...] + vy_buf[...]
    for j in range(1, height):
        vec_owner(j).start()
    for k in turns[:3]:
        settle(chunk[1][:1], k)
    total = vs_buf[...]
    for j in range(1, height):
        vec_owner(j).wait_recv()
        total = total + vz_buf[j - 1]
    vd_buf[...] = total
    for j in range(1, n_t):
        vec_peer(j).start()
    for k in turns[:3]:
        settle(chunk[1][1:], k)
    own = tok_in[...].astype(f32)
    own_normed, inv_std = norm_of(own)
    grad_normed = part_sum(1) * gain_a[...] + part_sum(2) * gain_m[...]
    x_ref[...] = grad_rows + inv_std * (
        grad_normed
        - jnp.mean(grad_normed, axis=-1, keepdims=True)
        - own_normed * jnp.mean(grad_normed * own_normed, axis=-1, keepdims=True)
    )
    y_ref[...] = own + part_sum(0) + b_dense[...] + b_down[...]
    total = vd_buf[...]
    for k in range(1, n_t):
        vec_peer(k).wait_recv()
        total = total + vt_buf[k - 1]
    owned = jnp.zeros((8, share), f32)
    for d in range(n_dp):
        owned = jnp.where(dp == d, total[:, d * share : (d + 1) * share], owned)
    vec_out[...] = owned
    qkv_bias_out[...] = vd_buf[5:6, :heads_wide]
    up_bias_out[...] = vd_buf[6:7, : w_up_in.shape[1]]
    close(chunk[0])
    close(chunk[1])

    for i in range(2):
        row_copy(rows_in[i], i, 0, t, over).wait_send()
        row_copy(rows_in[i], i, 1, t, twin).wait_send()
        row_copy(rows_in[i], i, 2, t, twin).wait_send()
    for a in everything:
        for step in range(height - 1):

            @pl.when((z - step >= 0) & has_right)
            def _(a=a, step=step):
                line(w_in[a], a, z, step, r_send, r_recv, right).wait_send()
                line_b(a, z, step, rb_send, rb_recv, right).wait_send()

            @pl.when((z + step < height) & has_left)
            def _(a=a, step=step):
                line(w_in[a], a, z, step, l_send, l_recv, left).wait_send()
                line_b(a, z, step, lb_send, lb_recv, left).wait_send()

        across_own(a, y).wait_send()
        for block in range(height):

            @pl.when(z != block)
            def _(a=a, block=block):
                across(a, block, y).wait_send()

        for k in range(height):
            swap(a, k).wait_send()
        for k in range(3):
            to_owner(a, k, 0).wait_send()
    vec_swap.wait_send()
    for k in range(1, height):
        vec_owner(k).wait_send()
    for k in range(1, n_t):
        vec_peer(k).wait_send()
    for i in range(3):
        to_twin(i).wait_send()
        to_over(i).wait_send()


def fused_layer(weights, rows, vectors, tables, n_dp, n_t):
    height = n_dp // PAIR
    bf16, f32 = jnp.bfloat16, jnp.float32
    group, width = rows[0].shape
    seq = group * n_t
    share = weights[0].shape[0]
    extra = share // 48 * 16
    heads_wide = weights[2].shape[1]
    wide = -(-heads_wide // 128) * 128
    units = weights[0].shape[1]
    cuts = (0, units // 3, units)
    n_vec = max(width, heads_wide, units)
    vmem = pl.BlockSpec(memory_space=pltpu.VMEM)
    dma = pltpu.SemaphoreType.DMA
    n_vs = height + n_t - 1
    widths = [heads_wide + weights[3].shape[0]]
    for c in range(len(cuts) - 1):
        widths += [cuts[c + 1] - cuts[c]] * 2
    n_p = len(widths)

    def buf(*shape, dtype=bf16):
        return pltpu.VMEM(shape, dtype)

    def per_piece(*lead):
        return [buf(*lead, w) for w in widths]

    def kernel(*refs):
        fused_kernel(n_dp, n_t, cuts, extra, refs)

    return pl.pallas_call(
        kernel,
        out_shape=[jax.ShapeDtypeStruct((group, width), f32)] * 2
        + [jax.ShapeDtypeStruct(w.shape, f32) for w in weights]
        + [
            jax.ShapeDtypeStruct((8, share), f32),
            jax.ShapeDtypeStruct((1, heads_wide), f32),
            jax.ShapeDtypeStruct((1, units), f32),
        ],
        in_specs=[vmem] * 16,
        out_specs=[vmem] * 9,
        scratch_shapes=per_piece(n_dp, share)
        + per_piece(n_dp, share)
        + per_piece(height, share)
        + per_piece(height - 1, share)
        + per_piece(2, share)
        + per_piece(2, share)
        + [buf(n_t, group, width)] * 2
        + [buf(2, 2, group, width)] * 3
        + [buf(2, group, width)] * 3
        + [buf(group, width)] * 6
        + [
            buf(8, n_vec, dtype=f32),
            buf(8, n_vec, dtype=f32),
            buf(8, n_vec, dtype=f32),
            buf(height - 1, 8, n_vec, dtype=f32),
            buf(8, n_vec, dtype=f32),
            buf(n_t - 1, 8, n_vec, dtype=f32),
            buf(seq, width, dtype=f32),
            buf(seq, width),
            buf(seq, width),
            buf(width, seq),
            buf(width, seq),
            buf(width, seq),
            buf(seq, units),
            buf(seq, units),
            buf(seq, wide, dtype=f32),
            buf(seq, wide, dtype=f32),
            buf(seq, wide, dtype=f32),
            buf(seq, wide, dtype=f32),
            buf(share, widths[0]),
            buf(share, widths[0], dtype=f32),
        ]
        + [dma((n_p, height - 1))] * 8
        + [dma((n_p, height))] * 2
        + [dma((n_p, height))] * 2
        + [dma((n_p, height - 1))]
        + [dma((n_p, 2))] * 2
        + [dma((2, 3))] * 2
        + [dma((3, 2))] * 2
        + [dma((n_vs,))] * 2,
        compiler_params=pltpu.CompilerParams(
            collective_id=2, has_side_effects=True, vmem_limit_bytes=63 * 1024 * 1024
        ),
        name="fused_layer",
    )(*weights, *rows, *vectors, *tables)


def hand_on(results, n_copied):
    hbm = pl.BlockSpec(memory_space=pl.ANY)
    large, vec = results[:n_copied], results[n_copied]
    share = vec.shape[1]
    rows = (0, 1, 2, 3, 4, 4)

    def kernel(*refs):
        n_in, n_out = n_copied + 1, n_copied + len(rows)
        ins_from, outs_to = refs[:n_in], refs[n_in : n_in + n_out]
        held = refs[n_in + n_out : -2]
        in_sem, out_sem = refs[-2:]
        ins = [pltpu.make_async_copy(ins_from[i], held[i], in_sem.at[i]) for i in range(n_in)]
        outs = [
            pltpu.make_async_copy(held[i], outs_to[i], out_sem.at[i]) for i in range(n_copied)
        ] + [
            pltpu.make_async_copy(
                held[n_copied].at[pl.ds(row, 1)], outs_to[n_copied + i], out_sem.at[n_copied + i]
            )
            for i, row in enumerate(rows)
        ]
        for copy in ins:
            copy.start()
        ins[n_copied].wait()
        for copy in outs[n_copied:]:
            copy.start()
        for i in range(n_copied):
            ins[i].wait()
            outs[i].start()
        for copy in outs:
            copy.wait()

    return pl.pallas_call(
        kernel,
        out_shape=[jax.ShapeDtypeStruct(r.shape, r.dtype) for r in large]
        + [jax.ShapeDtypeStruct((1, share), vec.dtype) for _ in rows],
        in_specs=[hbm] * (n_copied + 1),
        out_specs=[hbm] * (n_copied + len(rows)),
        scratch_shapes=[pltpu.VMEM(r.shape, r.dtype) for r in results]
        + [
            pltpu.SemaphoreType.DMA((n_copied + 1,)),
            pltpu.SemaphoreType.DMA((n_copied + len(rows),)),
        ],
        name="hand_on",
    )(*results)


def contract_rows(left, right):
    return dot(left, right, ((0,), (0,)))


def contract_cols(left, right):
    return dot(left, right, ((1,), (1,)))


def rotary_tables(pos_ids):
    half_rot = ROT // 2
    inverse = 10000.0 ** (-(jnp.arange(half_rot, dtype=jnp.float32) * 2.0) / ROT)
    angles = pos_ids.astype(jnp.float32)[:, None] * inverse[None, :]
    cos_tab = jnp.concatenate([jnp.cos(angles), jnp.cos(angles)], axis=-1)
    sine_tab = jnp.concatenate([jnp.sin(angles), jnp.sin(angles)], axis=-1)
    return (cos_tab, sine_tab)


def rotate(blocked, cos_tab, sine_tab):
    head_part = blocked[..., :ROT]
    low_half = head_part[..., : ROT // 2]
    high_half = head_part[..., ROT // 2 :]
    turned = jnp.concatenate([-high_half, low_half], axis=-1)
    spun_part = head_part * cos_tab[:, None, :] + turned * sine_tab[:, None, :]
    return jnp.concatenate([spun_part, blocked[..., ROT:]], axis=-1)


def unrotate(grad_part, cos_tab, sine_tab):
    head_part = grad_part[..., :ROT]
    scaled = head_part * sine_tab[:, None, :]
    back_turn = jnp.concatenate([scaled[..., ROT // 2 :], -scaled[..., : ROT // 2]], axis=-1)
    return jnp.concatenate(
        [head_part * cos_tab[:, None, :] + back_turn, grad_part[..., ROT:]], axis=-1
    )


def gelu_pair(pre_act):
    cdf = 0.5 * (1.0 + lax.erf(pre_act / math.sqrt(2.0)))
    pdf = jnp.exp(-0.5 * pre_act * pre_act) / math.sqrt(2.0 * math.pi)
    return pre_act * cdf, cdf + pre_act * pdf


def normalise(rows):
    center = rows - jnp.mean(rows, axis=-1, keepdims=True)
    inv_std = lax.rsqrt(jnp.mean(center * center, axis=-1, keepdims=True) + norm_eps)
    return center * inv_std, inv_std


def heads_einsum(spec, left, right):
    return jnp.einsum(spec, left, right, preferred_element_type=jnp.float32)


def shards(
    tokens,
    segments,
    positions,
    ln1_gain,
    ln1_bias,
    ln2_gain,
    ln2_bias,
    qkv_weight,
    qkv_bias,
    dense_weight,
    dense_bias,
    fc1_weight,
    fc1_bias,
    fc2_weight,
    fc2_bias,
    cotangent,
    *,
    n_dp,
    n_t,
):
    bf16 = jnp.bfloat16
    width = tokens.shape[1]
    group = tokens.shape[0]
    share = width // n_dp
    heads_wide = qkv_weight.shape[2]
    if share % 48 == 0 and heads_wide % 128 == 64 and heads_wide % 9 == 0 and n_t == 4 and n_dp == 4 * PAIR and fc1_weight.shape[2] % 768 == 0:
        fused = fused_layer(
            (fc1_weight[0], fc2_weight[0].T, qkv_weight[0], dense_weight[0]),
            (tokens, cotangent),
            (ln1_gain, ln1_bias, ln2_gain, ln2_bias, qkv_bias, fc1_bias, dense_bias, fc2_bias),
            (segments[None, :], positions[None, :]),
            n_dp,
            n_t,
        )
        y_out, x_grad, g_up, g_down_t, g_qkv, g_dense, sum_qkv, sum_up, *owned = hand_on(
            (*fused[:6], *fused[7:9], fused[6]), 8
        )
        return (
            y_out,
            x_grad,
            *owned[:4],
            g_qkv[None],
            sum_qkv,
            g_dense[None],
            owned[4],
            g_up[None],
            sum_up,
            g_down_t.T[None],
            owned[5],
        )
    gain_a, bias_a, gain_m, bias_m = ln1_gain[0], ln1_bias[0], ln2_gain[0], ln2_bias[0]
    gathered = gather_all(
        (qkv_weight[0], dense_weight[0].T, fc1_weight[0], fc2_weight[0].T),
        (tokens, cotangent),
        n_dp,
        n_t,
    )
    w_qkv, w_dense_t, w_up, w_down_t = [g.reshape(width, -1) for g in gathered[:4]]
    seq_rows, grad_full = [g.reshape(n_t * group, width) for g in gathered[4:]]
    seq_len = seq_rows.shape[0]

    cos_tab, sine_tab = rotary_tables(positions)
    normed, _ = normalise(seq_rows.astype(jnp.float32))
    in_attn = (normed * gain_a + bias_a).astype(bf16)
    in_mlp = (normed * gain_m + bias_m).astype(bf16)

    joined = (dot(in_attn, w_qkv, ((1,), (0,))) + qkv_bias[0]).reshape(seq_len, -1, 3, HEAD_DIM)
    queries = rotate(joined[:, :, 0], cos_tab, sine_tab).astype(bf16)
    key_rows = rotate(joined[:, :, 1], cos_tab, sine_tab).astype(bf16)
    value_rows = joined[:, :, 2].astype(bf16)

    score_scale = HEAD_DIM ** (-0.5)
    places_in = jnp.arange(seq_len, dtype=jnp.int32)
    allowed = (
        (segments[:, None] == segments[None, :]) & (places_in[:, None] >= places_in[None, :])
    )[None]
    scores = heads_einsum("qhd,khd->hqk", queries, key_rows) * score_scale
    scores = jnp.where(allowed, scores, -1e30)
    row_max = jnp.max(scores, axis=-1, keepdims=True)
    row_total = jnp.sum(jnp.exp(scores - row_max), axis=-1, keepdims=True)
    log_total = row_max + jnp.log(row_total)
    prob_wide = jnp.where(allowed, jnp.exp(scores - log_total), 0.0)
    probs = prob_wide.astype(bf16)
    context = heads_einsum("hqk,khd->qhd", probs, value_rows).reshape(seq_len, -1).astype(bf16)

    pre_act = dot(in_mlp, w_up, ((1,), (0,))) + fc1_bias[0]
    hidden, slope = gelu_pair(pre_act)
    hidden = hidden.astype(bf16)
    branch = contract_cols(context, w_dense_t) + contract_cols(hidden, w_down_t)

    grad_w_dense_t = contract_rows(grad_full, context)
    grad_w_down_t = contract_rows(grad_full, hidden)
    grad_pre = dot(grad_full, w_down_t, ((1,), (0,))) * slope
    grad_b_up = jnp.sum(grad_pre, axis=0)
    grad_pre_bf = grad_pre.astype(bf16)
    grad_ctx = dot(grad_full, w_dense_t, ((1,), (0,))).astype(bf16).reshape(seq_len, -1, HEAD_DIM)
    grad_w_up = contract_rows(in_mlp, grad_pre_bf)

    grad_probs = heads_einsum("qhd,khd->hqk", grad_ctx, value_rows)
    row_dot = jnp.sum(prob_wide * grad_probs, axis=-1, keepdims=True)
    grad_scores = (prob_wide * (grad_probs - row_dot) * score_scale).astype(bf16)
    grad_q = heads_einsum("hqk,khd->qhd", grad_scores, key_rows)
    grad_k = heads_einsum("hqk,qhd->khd", grad_scores, queries)
    grad_v = heads_einsum("hqk,qhd->khd", probs, grad_ctx)
    grad_joined = jnp.stack(
        [unrotate(grad_q, cos_tab, sine_tab), unrotate(grad_k, cos_tab, sine_tab), grad_v], axis=2
    ).reshape(seq_len, -1)
    grad_b_qkv = jnp.sum(grad_joined, axis=0)
    grad_joined_bf = grad_joined.astype(bf16)
    grad_w_qkv = contract_rows(in_attn, grad_joined_bf)

    part_attn = contract_cols(grad_joined_bf, w_qkv)
    part_mlp = contract_cols(grad_pre_bf, w_up)
    grad_rows = cotangent.astype(jnp.float32)
    heads_wide = grad_b_qkv.shape[0]
    n_vec = max(width, heads_wide, grad_b_up.shape[0])

    def lane(v):
        return jnp.pad(v, (0, n_vec - v.shape[0]))

    vec = jnp.stack(
        [
            lane(jnp.sum(part_attn * normed, axis=0)),
            lane(jnp.sum(part_attn, axis=0)),
            lane(jnp.sum(part_mlp * normed, axis=0)),
            lane(jnp.sum(part_mlp, axis=0)),
            lane(jnp.sum(grad_rows, axis=0)),
            lane(grad_b_qkv),
            lane(grad_b_up),
            jnp.zeros((n_vec,), jnp.float32),
        ]
    )

    def blocks(grad):
        return grad.astype(bf16).reshape(n_dp, width // n_dp, -1)

    def groups(part):
        return part.astype(bf16).reshape(n_t, group, width)

    (g_qkv, g_dense_t, g_up, g_down_t, mixed, grad_in_attn, grad_in_mlp, vec_sums) = reduce_all(
        (blocks(grad_w_qkv), blocks(grad_w_dense_t), blocks(grad_w_up), blocks(grad_w_down_t)),
        (groups(branch), groups(part_attn), groups(part_mlp)),
        vec,
        n_dp,
        n_t,
    )

    own_rows = tokens.astype(jnp.float32)
    own_normed, inv_std = normalise(own_rows)
    y_out = own_rows + mixed + dense_bias[0] + fc2_bias[0]
    grad_normed = grad_in_attn * gain_a + grad_in_mlp * gain_m
    x_grad = grad_rows + inv_std * (
        grad_normed
        - jnp.mean(grad_normed, axis=-1, keepdims=True)
        - own_normed * jnp.mean(grad_normed * own_normed, axis=-1, keepdims=True)
    )
    share = width // n_dp
    owned = lax.dynamic_slice_in_dim(vec_sums[1], lax.axis_index("dp") * share, share, axis=1)
    return (
        y_out,
        x_grad,
        owned[0:1],
        owned[1:2],
        owned[2:3],
        owned[3:4],
        g_qkv[None],
        vec_sums[0, 5:6, :heads_wide],
        g_dense_t.T[None],
        owned[4:5],
        g_up[None],
        vec_sums[0, 6:7, : grad_b_up.shape[0]],
        g_down_t.T[None],
        owned[4:5],
    )


def solution(mesh):
    placed = (
        P(("dp", "tensor"), None),
        P("dp"),
        P("dp"),
        P(),
        P(),
        P(),
        P(),
        P(None, "dp", "tensor"),
        P(None, "tensor"),
        P(None, "tensor", "dp"),
        P(),
        P(None, "dp", "tensor"),
        P(None, "tensor"),
        P(None, "tensor", "dp"),
        P(),
        P(("dp", "tensor"), None),
    )

    def step(*args):
        return shards(*args, n_dp=mesh.shape["dp"], n_t=mesh.shape["tensor"])

    return jax.shard_map(
        step,
        mesh=mesh,
        in_specs=placed,
        out_specs=(
            P(("dp", "tensor"), None),
            P(("dp", "tensor"), None),
            P(None, "dp"),
            P(None, "dp"),
            P(None, "dp"),
            P(None, "dp"),
            P(None, "dp", "tensor"),
            P(None, "tensor"),
            P(None, "tensor", "dp"),
            P(None, "dp"),
            P(None, "dp", "tensor"),
            P(None, "tensor"),
            P(None, "tensor", "dp"),
            P(None, "dp"),
        ),
        check_vma=False,
    )
```
